32 devices in a mesh: groups: 2 (over y), dom: 8 (over z, x), sub: 2 (over core).
Axes of the slice: x: 2, y: 2, z: 4, core: 2. Of those that a mesh axis runs over, the one named last changes fastest.
Arguments:
- right_sides: float32 [512, 1024], P(('groups', 'dom', 'sub')), parts along dimension 0
- diag_blocks: float32 [512, 64, 64], P(('groups', 'dom', 'sub')), parts along dimension 0
- off_blocks: float32 [512, 6, 64, 64], P(('groups', 'dom', 'sub')), parts along dimension 0, may hold values from -0.12 to 0.12
- stiffness: float32 [512, 6], P(('groups', 'dom', 'sub')), parts along dimension 0, may hold values from 0.5 to 2
- columns: int32 [512, 6], P(('groups', 'dom', 'sub')), parts along dimension 0, may hold values from 0 to 47, as said below
- interface: int32 [16, 2, 8], P(('groups', 'dom')), parts along dimension 0, may hold values from 0 to 31, as said below
- displacement: float32 [512, 64], P(('groups', 'dom', 'sub')), parts along dimension 0, may hold values from -6 to 6
- owners: int32 [3072, 1], P(('groups', 'dom', 'sub')), parts along dimension 0, may hold values from 0 to 7; in each aligned block of 96 rows (0 to 95, 96 to 191, ...) at most 14 rows name the same one
- generator_slot: int32 [3072, 1], P(('groups', 'dom', 'sub')), parts along dimension 0, may hold values from 0 to 127
Outputs:
- adjoint: float32 [512, 1024], P(('groups', 'dom', 'sub')), parts along dimension 0
- gen_grad: float32 [2048, 16], P(('groups', 'dom')), parts along dimension 0
The draws below stay inside these ranges and needn't reach their ends.
There are 2 independent parts, one for each index of `groups`. The reference program is written for one: setup_inputs(seed, part) draws one part's arguments, and reference() takes and returns one part's arrays. A program takes and returns all parts, laid end to end along the dimension named above; each array names one. Nothing has to cross between parts.
Inputs may be any that keep to these rules, and one draw needn't show every extreme that they name: `columns`: entries 0 to 3 of every block row lie in its own partition; entry 4 names a value of 32 or more (a row from partition p - 1) and entry 5 a value of 40 or more (a row from partition p + 1) wherever those partitions exist, and a row of the own partition otherwise. interface[p, 0] and interface[p, 1] each list 8 different block rows of partition p, numbered from 0 within the partition. `owners`: among the elements of the block rows of one device no partition is named more than 14 times.
All inputs are finite; a program needn't handle non-finite values.
Results may differ from the reference program's by a relative error of at most 0.0045.
Values sent between devices are 32-bit elements; how exact they have to be, the bound alone decides.
A program may use at most 64 MiB of HBM per device.

```python
import math
import jax
import jax.numpy as jnp
import numpy as np
from jax import lax

B = 64
R = 16
NBR = 16
ITERS = 2
GEN_DEV = 128
PART_ROWS = 32
IF = 8
ROWS = 256
ELEMS = 1536
CAP = 14
GENS = 1024
N_DOM = 8


def draw_right_sides(key, part):
    key_a, key_b, key_c = jax.random.split(key, 3)
    partition = (jnp.arange(ROWS) // PART_ROWS).astype(jnp.float32)
    row_ramp = 1.0 + 2.0 * partition / max(N_DOM - 1, 1)
    roughness = jax.random.uniform(key_b, (ROWS,), minval=0.5, maxval=1.5)
    col_scale = jnp.exp(jax.random.uniform(key_c, (R,), minval=jnp.log(0.3), maxval=jnp.log(3.0)))
    entries = jax.random.normal(key_a, (ROWS, B, R), dtype=jnp.float32)
    values = entries * (row_ramp * roughness)[:, None, None] * col_scale[None, None, :]
    return values.reshape(ROWS, B * R).astype(jnp.float32)


def draw_diag_blocks(key, part):
    key_a, key_b = jax.random.split(key, 2)
    partition = jnp.arange(ROWS, dtype=jnp.int32) // PART_ROWS
    level_factor = jnp.where(partition < N_DOM // 2, 8.0, 1.0).astype(jnp.float32)
    diag_level = jax.random.uniform(key_a, (ROWS, B), minval=1.5, maxval=3.0) * level_factor[:, None]
    entries = 0.01 * jax.random.normal(key_b, (ROWS, B, B), dtype=jnp.float32)
    identity = jnp.eye(B, dtype=jnp.float32)
    return (entries + identity[None, :, :] * diag_level[:, :, None]).astype(jnp.float32)


def draw_columns(key, part):
    key_a, key_b, key_c, key_d = jax.random.split(key, 4)
    partition = (jnp.arange(ROWS, dtype=jnp.int32) // PART_ROWS)[:, None]
    inner = jax.random.randint(key_a, (ROWS, 4), 0, PART_ROWS, dtype=jnp.int32)
    low_side = jax.random.randint(key_b, (ROWS, 1), 0, IF, dtype=jnp.int32) + PART_ROWS
    high_side = jax.random.randint(key_c, (ROWS, 1), 0, IF, dtype=jnp.int32) + PART_ROWS + IF
    fallback = jax.random.randint(key_d, (ROWS, 2), 0, PART_ROWS, dtype=jnp.int32)
    low_side = jnp.where(partition == 0, fallback[:, :1], low_side)
    high_side = jnp.where(partition == N_DOM - 1, fallback[:, 1:], high_side)
    return jnp.concatenate([inner, low_side, high_side], axis=1).astype(jnp.int32)


def draw_interface(key, part):
    scores = jax.random.randint(key, (N_DOM, 2, PART_ROWS), 0, 2 ** 20, dtype=jnp.int32)
    scores = scores * PART_ROWS + jnp.arange(PART_ROWS, dtype=jnp.int32)[None, None, :]
    ordering = jnp.argsort(scores, axis=-1, stable=True)
    return ordering[:, :, :IF].astype(jnp.int32)


def plant(values, stream_key, low, largest):
    index_at = [jax.random.randint(jax.random.fold_in(stream_key, axis), (), 0, length) for axis, length in enumerate(values.shape)]
    widest = values.shape.index(max(values.shape))
    beside = index_at[:widest] + [(index_at[widest] + 1) % values.shape[widest]] + index_at[widest + 1:]
    return values.at[tuple(index_at)].set(low).at[tuple(beside)].set(largest)


def level_of(key, extent, cuts, least, top_value):
    def one(dim, shards_of):
        heights = jax.random.uniform(jax.random.fold_in(jax.random.fold_in(key, 6), dim), (shards_of,), jnp.float32, least / len(cuts), top_value / len(cuts))
        return jnp.repeat(jnp.exp(heights), extent[dim] // shards_of).reshape((-1,) + (1,) * (len(extent) - dim - 1))

    level = one(*cuts[0])
    for cut in cuts[1:]:
        level = level * one(*cut)
    return level


def assign_block(key, own, number, rows, count, top, bound, skew):
    sequence = jax.random.permutation(key, count)
    crowded, ordinary = portions_of(count, rows * top, bound, skew, True), portions_of(count, rows * top, bound, skew, False)
    places = jnp.arange(count)

    def named(lengths, turn):
        used = int((lengths > 0).sum())
        fixed = max(1, used // 4)
        passed = fixed + (places - fixed + turn * (used - fixed)) % max(1, count - fixed)
        return jnp.zeros((count,), jnp.int32).at[sequence[jnp.where(places < fixed, places, passed)]].set(jnp.asarray(lengths, jnp.int32))

    lengths = jnp.where(number % 4 == 0, named(crowded, number // 4), named(ordinary, number - number // 4 - 1))
    mixed = jax.random.permutation(jax.random.fold_in(own, 3), count)
    source_of, receiver = mixed[0:count // 2 * 2:2], mixed[1:count // 2 * 2:2]
    slack = jnp.minimum(lengths[source_of] - 1, bound - lengths[receiver]) // 2
    slack = jnp.where((source_of == sequence[0]) | (receiver == sequence[0]) | (lengths[receiver] == 0), 0, jnp.maximum(slack, 0))
    passed = jax.random.randint(jax.random.fold_in(own, 4), (count // 2,), 0, 1 << 20) % (slack + 1)
    lengths = lengths.at[source_of].add(-passed).at[receiver].add(passed)
    items = jnp.searchsorted(jnp.cumsum(lengths), jnp.arange(rows * top), side="right").astype(jnp.int32)
    table = items.reshape(top, rows).T
    table = table[jax.random.permutation(jax.random.fold_in(own, 1), rows)]
    turn = jax.random.randint(jax.random.fold_in(own, 2), (rows, 1), 0, top)
    return jnp.take_along_axis(table, (jnp.arange(top)[None, :] + turn) % top, axis=1)


def portions_of(amount, total, most, slope, full):
    loads = [(1 << 20) // math.isqrt(grade ** slope) + 1 for grade in range(1, amount + 1)]
    largest = most if full else min(most, max(-(-total // amount), total * loads[0] // sum(loads)))
    least = 1 if total - largest >= amount - 1 else 0
    holding, rest = [largest] + [least] * (amount - 1), total - largest - least * (amount - 1)
    while rest > 0:
        candidates = [i for i in range(1, amount) if holding[i] < largest] or [i for i in range(1, amount) if holding[i] < most]
        pool, left = sum([loads[i] for i in candidates]), rest
        for i in candidates:
            addition = min(most - holding[i], max(1, left * loads[i] // pool), rest)
            holding[i] = holding[i] + addition
            rest = rest - addition
    return np.array(holding)


def gaussian(key, shape, scale, reach, cuts=(), kind=jnp.bfloat16):
    values = jax.random.normal(key, shape, jnp.float32) * scale
    if len(cuts) > 0:
        values = level_of(key, shape, cuts, -0.22, 0.18) * values
    return jnp.clip(values, min=-reach, max=reach).astype(kind)


def setup_inputs(seed: int = 0, part: int = 0) -> dict:
    keys = jax.random.split(jax.random.key(seed), 10)
    own_keys = jax.random.split(jax.random.fold_in(keys[9], part), 10)
    right_sides = draw_right_sides(jax.random.fold_in(jax.random.fold_in(keys[9], part), 71), part)
    diag_blocks = draw_diag_blocks(jax.random.fold_in(jax.random.fold_in(keys[9], part), 71), part)
    off_blocks = gaussian(own_keys[2], (ROWS, 6, B, B), 0.02, 0.12, ((0, 16),), jnp.float32)
    stiffness = jnp.clip(jnp.exp(math.log(2.0) - 1.3862944 * jax.random.uniform(own_keys[3], (ROWS, 6), jnp.float32) ** level_of(own_keys[3], (ROWS, 6), ((0, 16),), -0.2, 0.2)), 0.5, 2.0)
    columns = draw_columns(jax.random.fold_in(jax.random.fold_in(keys[9], part), 71), part)
    interface = draw_interface(jax.random.fold_in(jax.random.fold_in(keys[9], part), 71), part)
    displacement = gaussian(own_keys[6], (ROWS, B), 1.0, 6.0, ((0, 16),), jnp.float32)
    owners_keys = jax.random.split(jax.random.fold_in(own_keys[7], 1), ELEMS // (NBR * 6))
    owners_turns = jax.random.permutation(jax.random.fold_in(own_keys[7], 3), ELEMS // (NBR * 6))
    owners = jax.vmap(lambda own, number: assign_block(jax.random.fold_in(own_keys[7], 2), own, number, NBR * 6, N_DOM, 1, CAP, 1))(owners_keys, owners_turns).reshape((ELEMS, 1))
    generator_slot = plant(jax.random.randint(own_keys[8], (ELEMS, 1), 0, GEN_DEV), jax.random.fold_in(own_keys[8], 1), 0, GEN_DEV - 1).astype(jnp.int32)
    return dict(right_sides=right_sides, diag_blocks=diag_blocks, off_blocks=off_blocks, stiffness=stiffness, columns=columns, interface=interface, displacement=displacement, owners=owners, generator_slot=generator_slot)


def global_columns(columns, interface):
    row_count = columns.shape[0]
    partition = (jnp.arange(row_count, dtype=jnp.int32) // PART_ROWS)[:, None]
    lower = jnp.maximum(partition - 1, 0)
    upper = jnp.minimum(partition + 1, N_DOM - 1)
    low_index = jnp.clip(columns - PART_ROWS, 0, IF - 1).astype(jnp.int32)
    high_index = jnp.clip(columns - PART_ROWS - IF, 0, IF - 1).astype(jnp.int32)
    from_lower = lower * PART_ROWS + interface[lower, 1, low_index]
    from_upper = upper * PART_ROWS + interface[upper, 0, high_index]
    inside = partition * PART_ROWS + columns
    chosen = jnp.where(columns < PART_ROWS, inside, jnp.where(columns < PART_ROWS + IF, from_lower, from_upper))
    return chosen.astype(jnp.int32)


def apply_matrix(vector, diag_blocks, off_blocks, stiffness, where_cols):
    blocks = vector.reshape(-1, B, R)
    picked = blocks[where_cols] * stiffness[:, :, None, None]
    result = jnp.einsum("nab,nbr->nar", diag_blocks, blocks, precision=lax.Precision.HIGHEST)
    result = result + jnp.einsum("nkab,nkbr->nar", off_blocks, picked, precision=lax.Precision.HIGHEST)
    return result.reshape(vector.shape)


def column_sums(left_rows, right_rows):
    return jnp.sum((left_rows * right_rows).reshape(-1, B, R), axis=(0, 1))


def spread(per_column):
    return jnp.tile(per_column, B)[None, :]


def reference(right_sides, diag_blocks, off_blocks, stiffness, columns, interface, displacement, owners, generator_slot):
    where_cols = global_columns(columns, interface)
    adjoint = jnp.zeros_like(right_sides)
    residual = right_sides
    direction = right_sides
    norm_now = column_sums(residual, residual)
    for step in range(ITERS):
        applied = apply_matrix(direction, diag_blocks, off_blocks, stiffness, where_cols)
        step_size = norm_now / column_sums(direction, applied)
        adjoint = adjoint + spread(step_size) * direction
        residual = residual - spread(step_size) * applied
        if step + 1 < ITERS:
            norm_next = column_sums(residual, residual)
            direction = residual + spread(norm_next / norm_now) * direction
            norm_now = norm_next
    state_cols = displacement[where_cols]
    pushed = jnp.einsum("nkab,nkb->nka", off_blocks, state_cols, precision=lax.Precision.HIGHEST)
    element_grads = -jnp.einsum("nka,nar->nkr", pushed, adjoint.reshape(-1, B, R), precision=lax.Precision.HIGHEST)
    element_grads = element_grads * stiffness[:, :, None]
    element_grads = element_grads.reshape(-1, R)
    gen_ids = (owners[:, 0] * GEN_DEV + generator_slot[:, 0]).astype(jnp.int32)
    gen_grad = jax.ops.segment_sum(element_grads, gen_ids, num_segments=GENS)
    return adjoint, gen_grad
```

```python
import functools
import jax
import jax.numpy as jnp
from jax import lax
from jax.experimental import pallas as pl
from jax.experimental.pallas import tpu as pltpu
from jax.sharding import PartitionSpec as P

B = 64
R = 16
NBR = 16
NK = 6
IF = 8
GEN_DEV = 128
SLOTS = 16
CHUNK = 16
STEP = 4

F32 = jnp.float32
BF16 = jnp.bfloat16
MESH = pl.DeviceIdType.MESH
TRANS = (((1,), (1,)), ((), ()))


def iota(shape, dim):
    return lax.broadcasted_iota(jnp.int32, shape, dim)


def halves(x):
    hi = x.astype(BF16)
    lo = (x - hi.astype(F32)).astype(BF16)
    return hi, lo


def to_row(parts):
    lane = iota((8, 128), 1)
    sub = iota((8, 128), 0)
    low = lane < B
    out = jnp.zeros((8, 128), F32)
    for m, part in enumerate(parts):
        s0 = jnp.sum(jnp.where(low, part, 0.0), axis=1, keepdims=True)
        s1 = jnp.sum(jnp.where(low, 0.0, part), axis=1, keepdims=True)
        out = jnp.where(lane % 16 == 2 * m, s0, out)
        out = jnp.where(lane % 16 == 2 * m + 1, s1, out)
    out = jnp.where(sub == lane // 16, out, 0.0)
    return jnp.sum(out, axis=0, keepdims=True)


def from_row(row, count):
    lane = iota((8, 128), 1)
    sub = iota((8, 128), 0)
    own = jnp.where(sub == lane // 16, jnp.broadcast_to(row, (8, 128)), 0.0)
    res = []
    for m in range(count):
        s0 = jnp.sum(jnp.where(lane % 16 == 2 * m, own, 0.0), axis=1, keepdims=True)
        s1 = jnp.sum(jnp.where(lane % 16 == 2 * m + 1, own, 0.0), axis=1, keepdims=True)
        res.append(jnp.where(lane < B, s0, s1))
    return res


def kernel(n_dom, n_sub, stiff, cols, iface, b_ref, diag_ref, off_ref, u_ref, own_ref, slot_ref,
           adj_ref, gen_ref,
           wts, ext_b, ext_u, ext_q, q_ref, w_ref, u_own, sb, sq, rb, rq, grads, gmsg, rgr, ar1, ar2, row1, row2,
           s_part, r_part, s_halo, r_halo, s_a1, r_a1, s_a2, r_a2, s_g, r_g):
    dom = lax.axis_index("dom")
    sub = lax.axis_index("sub")
    count = n_dom * n_sub
    me = dom * n_sub + sub
    base = sub * NBR
    other = 1 - sub

    barrier = pltpu.get_barrier_semaphore()

    def greet(t, c):
        peer = lax.rem(me + t, count)
        pl.semaphore_signal(barrier, inc=1, device_id={"dom": peer // n_sub, "sub": lax.rem(peer, n_sub)},
                            device_id_type=MESH)
        return c

    lax.fori_loop(1, count, greet, 0)

    u = u_ref[...]
    u_own[...] = jnp.concatenate([u, u], axis=1)
    for way in range(2):
        for j in range(IF):
            local = iface[0, way, j] - base
            mine = (local >= 0) & (local < NBR)
            idx = jnp.clip(local, 0, NBR - 1)
            sb[way, j] = jnp.where(mine, b_ref[idx], 0.0)
            sb[way, IF, j:j + 1, :] = jnp.where(mine, u_own[pl.ds(idx, 1), :], 0.0)

    pl.semaphore_wait(barrier, count - 1)

    def partner(which):
        if which == 0:
            src, dst = b_ref, ext_b.at[pl.ds(base, NBR)]
        elif which == 1:
            src, dst = u_own, ext_u.at[pl.ds(base, NBR)]
        else:
            src, dst = q_ref, ext_q.at[pl.ds(base, NBR)]
        return pltpu.make_async_remote_copy(src_ref=src, dst_ref=dst, send_sem=s_part.at[which],
                                            recv_sem=r_part.at[which], device_id={"sub": other},
                                            device_id_type=MESH)

    def halo(phase, way, tsub, slot):
        src = (sb, sq)[phase]
        dst = (rb, rq)[phase]
        target = dom - 1 if way == 0 else dom + 1
        return pltpu.make_async_remote_copy(src_ref=src.at[way], dst_ref=dst.at[1 - way, slot],
                                            send_sem=s_halo.at[phase, way, tsub],
                                            recv_sem=r_halo.at[phase, 1 - way, slot],
                                            device_id={"dom": target, "sub": tsub}, device_id_type=MESH)

    def halo_each(phase, act):
        for way in range(2):
            ok = dom > 0 if way == 0 else dom < n_dom - 1

            @pl.when(ok)
            def _():
                for tsub in range(n_sub):
                    act(phase, way, tsub)

    def start_halo(phase):
        def go(phase, way, tsub):
            halo(phase, way, tsub, sub).start()
        halo_each(phase, go)

    def wait_halo_send(phase):
        def go(phase, way, tsub):
            halo(phase, way, tsub, sub).wait_send()
        halo_each(phase, go)

    def wait_halo(phase, ext):
        buf = (rb, rq)[phase]
        for side in range(2):
            there = dom > 0 if side == 0 else dom < n_dom - 1

            @pl.when(there)
            def _():
                for ssub in range(n_sub):
                    halo(phase, 1 - side, 0, ssub).wait_recv()
                lo = 2 * NBR + side * IF
                ext[lo:lo + IF] = buf[side, 0, :IF] + buf[side, 1, :IF]
                if phase == 0:
                    ext_u[lo:lo + IF, :] = buf[side, 0, IF] + buf[side, 1, IF]

            @pl.when(jnp.logical_not(there))
            def _():
                lo = 2 * NBR + side * IF
                ext[lo:lo + IF] = jnp.zeros((IF, 8, 128), F32)
                if phase == 0:
                    ext_u[lo:lo + IF, :] = jnp.zeros((IF, 128), F32)

    def row_copy(row, box, s_sem, r_sem, peer, slot):
        return pltpu.make_async_remote_copy(
            src_ref=row, dst_ref=box.at[slot], send_sem=s_sem.at[peer], recv_sem=r_sem.at[slot],
            device_id={"dom": peer // n_sub, "sub": lax.rem(peer, n_sub)}, device_id_type=MESH)

    def over_peers(act):
        def go(t, c):
            act(lax.rem(me + t, count))
            return c
        lax.fori_loop(1, count, go, 0)

    def start_row(row, box, s_sem, r_sem, value):
        row[...] = value
        over_peers(lambda peer: row_copy(row, box, s_sem, r_sem, peer, me).start())
        box[pl.ds(me, 1)] = value.reshape(1, 1, 128)

    def wait_row(row, box, s_sem, r_sem):
        over_peers(lambda peer: row_copy(row, box, s_sem, r_sem, peer, peer).wait_recv())
        return jnp.sum(box[...], axis=0)

    def wait_row_send(row, box, s_sem, r_sem):
        over_peers(lambda peer: row_copy(row, box, s_sem, r_sem, peer, me).wait_send())

    def grad_copy(peer, slot):
        return pltpu.make_async_remote_copy(
            src_ref=gmsg.at[pl.ds((peer // n_sub) * SLOTS, SLOTS)], dst_ref=rgr.at[slot],
            send_sem=s_g.at[peer], recv_sem=r_g.at[slot],
            device_id={"dom": peer // n_sub, "sub": lax.rem(peer, n_sub)}, device_id_type=MESH)

    partner(0).start()
    partner(1).start()
    start_halo(0)
    ext_b[pl.ds(base, NBR)] = b_ref[...]
    ext_u[pl.ds(base, NBR), :] = u_own[...]

    def prepare(n, c):
        blocks = [off_ref[n, k] * stiff[k, n] for k in range(NK)] + [diag_ref[n], jnp.zeros((B, B), F32)]
        hi, lo = halves(jnp.concatenate(blocks, axis=1))
        wts[n, :B, :] = hi
        wts[n, B:, :] = lo
        return c

    lax.fori_loop(0, NBR, prepare, 0)

    pr = iota((128, 128), 0)
    pc = iota((128, 128), 1)
    real_r = pr % 8 < NK
    source = jnp.where(real_r, NK * (pr // 8) + pr % 8, -1)[:, :NBR * NK]
    pick = (source == iota((128, NBR * NK), 1)).astype(BF16)
    pair = jnp.where(iota((16, NBR * NK), 0) == 0, jnp.broadcast_to(own_ref[...], (16, NBR * NK)),
                     jnp.broadcast_to(slot_ref[...], (16, NBR * NK)))
    pair = lax.dot_general(pair.astype(F32).astype(BF16), pick, TRANS, preferred_element_type=F32)
    own_row = jnp.where(pc[0:1] % 8 < NK, pair[0:1], -1.0)
    own_col = jnp.sum(jnp.where(pr == pc, own_row, 0.0), axis=1, keepdims=True)
    slot_col = jnp.sum(jnp.where(pr == pc, pair[1:2], 0.0), axis=1, keepdims=True)
    same = (own_col == own_row) & (pr < pc)
    rank_row = jnp.sum(jnp.where(same, 1.0, 0.0), axis=0, keepdims=True)
    dest_row = jnp.where(own_row >= 0.0, own_row * SLOTS + rank_row, -1.0)
    grads[...] = jnp.broadcast_to(slot_col + 1.0, (128, 128))

    lane = iota((8, 128), 1)
    row8 = iota((8, 128), 0)
    low = lane < B

    def gathered(ext, n):
        xs = [ext[cols[k, n]] for k in range(NK)]
        own = ext[base + n]
        pieces = []
        for p in range(NK // 2):
            x0, x1 = xs[2 * p], xs[2 * p + 1]
            top = jnp.where(low, x0, pltpu.roll(x1, B, 1))
            bot = jnp.where(low, pltpu.roll(x0, B, 1), x1)
            pieces.append(jnp.concatenate([top, bot], axis=0))
        own16 = jnp.concatenate([own, pltpu.roll(own, B, 1)], axis=0)
        pieces.append(jnp.where(iota((16, 128), 1) < B, own16, 0.0))
        return jnp.concatenate(pieces, axis=1), own16

    def first(n):
        x, own16 = gathered(ext_b, n)
        hi, lo = halves(x)
        us = [ext_u[pl.ds(cols[k, n], 1), :] for k in range(NK)]
        upieces = []
        for p in range(NK // 2):
            upieces.append(jnp.where((row8 == 2 * p) & low, us[2 * p],
                                     jnp.where((row8 == 2 * p + 1) & ~low, us[2 * p + 1], 0.0)))
        upieces.append(jnp.zeros((8, 128), F32))
        uu = jnp.concatenate(upieces, axis=1)
        uh = uu.astype(BF16).astype(F32)
        u16 = jnp.concatenate([uh, uu - uh], axis=0).astype(BF16)
        lhs = jnp.concatenate([hi, lo, u16], axis=0)
        out = lax.dot_general(lhs, wts[n], TRANS, preferred_element_type=F32)
        t = out[0:16] + out[16:32]
        t = t + pltpu.roll(t, B, 1)
        q_ref[n] = jnp.where(low, t[0:8], t[8:16])
        p = out[32:40] + out[40:48]
        p = jnp.where(low, p + pltpu.roll(p, B, 1), 0.0)
        v = jnp.concatenate([own16, t], axis=0)
        vh = v.astype(BF16)
        vl = (v - vh.astype(F32)).astype(BF16)
        ph = p.astype(BF16).astype(F32)
        p16 = jnp.concatenate([ph, p - ph], axis=0).astype(BF16)
        g = lax.dot_general(p16, jnp.concatenate([vh, vl], axis=0), TRANS, preferred_element_type=F32)
        g = g[0:8] + g[8:16]
        g = g[:, 0:32] + g[:, 32:64]
        grads[pl.ds(pl.multiple_of(n * 8, 8), 8), 0:32] = -g

    def second(n):
        x, _ = gathered(ext_q, n)
        hi, lo = halves(x)
        out = lax.dot_general(jnp.concatenate([hi, lo], axis=0), wts[n], TRANS, preferred_element_type=F32)
        t = out[0:16] + out[16:32]
        t = t + pltpu.roll(t, B, 1)
        w_ref[n] = jnp.where(low, t[0:8], t[8:16])

    def rows(body):
        def go(i, c):
            for j in range(STEP):
                body(i * STEP + j)
            return c
        lax.fori_loop(0, NBR // STEP, go, 0)

    partner(0).wait_recv()
    partner(1).wait_recv()
    wait_halo(0, ext_b)
    rows(first)

    for way in range(2):
        for j in range(IF):
            local = iface[0, way, j] - base
            mine = (local >= 0) & (local < NBR)
            sq[way, j] = jnp.where(mine, q_ref[jnp.clip(local, 0, NBR - 1)], 0.0)
    partner(2).start()
    start_halo(1)
    b = b_ref[...]
    q = q_ref[...]
    ext_q[pl.ds(base, NBR)] = q
    start_row(row1, ar1, s_a1, r_a1, to_row([jnp.sum(b * b, axis=0), jnp.sum(b * q, axis=0)]))

    gh, gl = halves(grads[...])
    for blk in range(n_dom * SLOTS // 128):
        pick2 = (dest_row == (pr + blk * 128).astype(F32)).astype(BF16)
        gmsg[blk * 128:(blk + 1) * 128, :] = (jnp.dot(pick2, gh, preferred_element_type=F32)
                                              + jnp.dot(pick2, gl, preferred_element_type=F32))
    over_peers(lambda peer: grad_copy(peer, me).start())
    rgr[pl.ds(me, 1)] = gmsg[pl.ds(pl.multiple_of(dom * SLOTS, SLOTS), SLOTS), :].reshape(1, SLOTS, 128)

    partner(2).wait_recv()
    wait_halo(1, ext_q)
    rows(second)

    rr, bq = from_row(wait_row(row1, ar1, s_a1, r_a1), 2)
    step1 = rr / bq
    w = w_ref[...]
    r1 = b - step1 * q
    a_r1 = q - step1 * w
    start_row(row2, ar2, s_a2, r_a2, to_row([jnp.sum(r1 * r1, axis=0), jnp.sum(r1 * a_r1, axis=0),
                                             jnp.sum(r1 * q, axis=0), jnp.sum(b * a_r1, axis=0)]))

    over_peers(lambda peer: grad_copy(peer, peer).wait_recv())
    acc = jnp.zeros((2 * R, GEN_DEV), F32)
    for blk in range(count // CHUNK):
        x = rgr[blk * CHUNK:(blk + 1) * CHUNK].reshape(CHUNK * SLOTS, 128)
        hot = (x[:, 32:33] == (iota((CHUNK * SLOTS, GEN_DEV), 1) + 1).astype(F32)).astype(BF16)
        xh, xl = halves(x.T[:2 * R])
        acc = acc + jnp.dot(xh, hot, preferred_element_type=F32) + jnp.dot(xl, hot, preferred_element_type=F32)

    new, m1, m2, m3 = from_row(wait_row(row2, ar2, s_a2, r_a2), 4)
    beta = new / rr
    step2 = new / (m1 + beta * (m2 + m3 + beta * bq))
    adj_ref[...] = step1 * b + step2 * (r1 + beta * b)
    c1 = step1 + step2 * (1.0 + beta)
    c2 = -step2 * step1
    c1 = jnp.concatenate([c1[:, 0:1], c1[:, B:B + 1]], axis=0)
    c2 = jnp.concatenate([c2[:, 0:1], c2[:, B:B + 1]], axis=0)
    gen_ref[...] = c1 * acc[:R] + c2 * acc[R:]

    partner(0).wait_send()
    partner(1).wait_send()
    partner(2).wait_send()
    wait_halo_send(0)
    wait_halo_send(1)
    wait_row_send(row1, ar1, s_a1, r_a1)
    wait_row_send(row2, ar2, s_a2, r_a2)
    over_peers(lambda peer: grad_copy(peer, me).wait_send())


def shards(right_sides, diag_blocks, off_blocks, stiffness, columns, interface, displacement, owners,
           generator_slot):
    n_dom = lax.axis_size("dom")
    n_sub = lax.axis_size("sub")
    count = n_dom * n_sub
    packed = right_sides.reshape(NBR, B, 2, 8).transpose(0, 3, 2, 1).reshape(NBR, 8, 128)
    smem = pl.BlockSpec(memory_space=pltpu.SMEM)
    vmem = pl.BlockSpec(memory_space=pltpu.VMEM)
    dma = pltpu.SemaphoreType.DMA
    ext = 2 * NBR + 2 * IF
    adj, gen = pl.pallas_call(
        functools.partial(kernel, n_dom, n_sub),
        out_shape=(jax.ShapeDtypeStruct((NBR, 8, 128), F32), jax.ShapeDtypeStruct((R, GEN_DEV), F32)),
        in_specs=[smem] * 3 + [vmem] * 6,
        out_specs=(vmem, vmem),
        scratch_shapes=[
            pltpu.VMEM((NBR, 2 * B, 8 * B), BF16),
            pltpu.VMEM((ext, 8, 128), F32),
            pltpu.VMEM((ext, 128), F32),
            pltpu.VMEM((ext, 8, 128), F32),
            pltpu.VMEM((NBR, 8, 128), F32),
            pltpu.VMEM((NBR, 8, 128), F32),
            pltpu.VMEM((NBR, 128), F32),
            pltpu.VMEM((2, IF + 1, 8, 128), F32),
            pltpu.VMEM((2, IF, 8, 128), F32),
            pltpu.VMEM((2, 2, IF + 1, 8, 128), F32),
            pltpu.VMEM((2, 2, IF, 8, 128), F32),
            pltpu.VMEM((128, 128), F32),
            pltpu.VMEM((n_dom * SLOTS, 128), F32),
            pltpu.VMEM((count, SLOTS, 128), F32),
            pltpu.VMEM((count, 1, 128), F32),
            pltpu.VMEM((count, 1, 128), F32),
            pltpu.VMEM((1, 128), F32),
            pltpu.VMEM((1, 128), F32),
            dma((3,)), dma((3,)),
            dma((2, 2, 2)), dma((2, 2, 2)),
            dma((count,)), dma((count,)),
            dma((count,)), dma((count,)),
            dma((count,)), dma((count,)),
        ],
        compiler_params=pltpu.CompilerParams(collective_id=0, has_side_effects=True,
                                             vmem_limit_bytes=40 * 1024 * 1024),
    )(stiffness.T, columns.T, interface, packed, diag_blocks, off_blocks, displacement, owners.T, generator_slot.T)
    adjoint = adj.reshape(NBR, 8, 2, B).transpose(0, 3, 2, 1).reshape(NBR, B * R)
    return adjoint, gen.T


def solution(mesh):
    in_specs = (
        P(("groups", "dom", "sub"), None),
        P(("groups", "dom", "sub"), None, None),
        P(("groups", "dom", "sub"), None, None, None),
        P(("groups", "dom", "sub"), None),
        P(("groups", "dom", "sub"), None),
        P(("groups", "dom"), None, None),
        P(("groups", "dom", "sub"), None),
        P(("groups", "dom", "sub"), None),
        P(("groups", "dom", "sub"), None),
    )
    out_specs = (P(("groups", "dom", "sub"), None), P(("groups", "dom"), None))
    return jax.shard_map(shards, mesh=mesh, in_specs=in_specs, out_specs=out_specs, check_vma=False)
```

```python
import functools
import jax
import jax.numpy as jnp
from jax import lax
from jax.experimental import pallas as pl
from jax.experimental.pallas import tpu as pltpu
from jax.sharding import PartitionSpec as P

B = 64
R = 16
NBR = 16
NK = 6
IF = 8
GEN_DEV = 128
SLOTS = 16
CHUNK = 16
STEP = 4

F32 = jnp.float32
BF16 = jnp.bfloat16
MESH = pl.DeviceIdType.MESH
TRANS = (((1,), (1,)), ((), ()))


def iota(shape, dim):
    return lax.broadcasted_iota(jnp.int32, shape, dim)


def halves(x):
    hi = x.astype(BF16)
    lo = (x - hi.astype(F32)).astype(BF16)
    return hi, lo


def to_row(parts):
    lane = iota((8, 128), 1)
    sub = iota((8, 128), 0)
    low = lane < B
    out = jnp.zeros((8, 128), F32)
    for m, part in enumerate(parts):
        s0 = jnp.sum(jnp.where(low, part, 0.0), axis=1, keepdims=True)
        s1 = jnp.sum(jnp.where(low, 0.0, part), axis=1, keepdims=True)
        out = jnp.where(lane % 16 == 2 * m, s0, out)
        out = jnp.where(lane % 16 == 2 * m + 1, s1, out)
    out = jnp.where(sub == lane // 16, out, 0.0)
    return jnp.sum(out, axis=0, keepdims=True)


def from_row(row, count):
    lane = iota((8, 128), 1)
    sub = iota((8, 128), 0)
    own = jnp.where(sub == lane // 16, jnp.broadcast_to(row, (8, 128)), 0.0)
    res = []
    for m in range(count):
        s0 = jnp.sum(jnp.where(lane % 16 == 2 * m, own, 0.0), axis=1, keepdims=True)
        s1 = jnp.sum(jnp.where(lane % 16 == 2 * m + 1, own, 0.0), axis=1, keepdims=True)
        res.append(jnp.where(lane < B, s0, s1))
    return res


def kernel(n_dom, n_sub, *refs):
    hbm, (b_ref, adj_ref, gen_ref), local, rest = refs[:8], refs[8:11], refs[11:19], refs[19:]
    l_sem = rest[-1]
    loads = [pltpu.make_async_copy(hbm[i], local[i], l_sem.at[i]) for i in range(8)]
    for load in loads:
        load.start()
    body(n_dom, n_sub, loads, *local, b_ref, adj_ref, gen_ref, *rest[:-1])


def body(n_dom, n_sub, loads, iface, u_ref, cols, stiff, diag_ref, off_ref, own_ref, slot_ref, b_ref,
         adj_ref, gen_ref,
           wts, ext_b, ext_u, ext_q, q_ref, w_ref, u_own, sb, sq, rb, rq, grads, gmsg, rgr, ar1, ar2, row1, row2,
           s_part, r_part, s_halo, r_halo, s_a1, r_a1, s_a2, r_a2, s_g, r_g):
    dom = lax.axis_index("dom")
    sub = lax.axis_index("sub")
    count = n_dom * n_sub
    me = dom * n_sub + sub
    base = sub * NBR
    other = 1 - sub

    barrier = pltpu.get_barrier_semaphore()

    def greet(t, c):
        peer = lax.rem(me + t, count)
        pl.semaphore_signal(barrier, inc=1, device_id={"dom": peer // n_sub, "sub": lax.rem(peer, n_sub)},
                            device_id_type=MESH)
        return c

    lax.fori_loop(1, count, greet, 0)

    loads[0].wait()
    loads[1].wait()
    u = u_ref[...]
    u_own[...] = jnp.concatenate([u, u], axis=1)
    for way in range(2):
        for j in range(IF):
            local = iface[0, way, j] - base
            mine = (local >= 0) & (local < NBR)
            idx = jnp.clip(local, 0, NBR - 1)
            sb[way, j] = jnp.where(mine, b_ref[idx], 0.0)
            sb[way, IF, j:j + 1, :] = jnp.where(mine, u_own[pl.ds(idx, 1), :], 0.0)

    pl.semaphore_wait(barrier, count - 1)

    def partner(which):
        if which == 0:
            src, dst = b_ref, ext_b.at[pl.ds(base, NBR)]
        elif which == 1:
            src, dst = u_own, ext_u.at[pl.ds(base, NBR)]
        else:
            src, dst = q_ref, ext_q.at[pl.ds(base, NBR)]
        return pltpu.make_async_remote_copy(src_ref=src, dst_ref=dst, send_sem=s_part.at[which],
                                            recv_sem=r_part.at[which], device_id={"sub": other},
                                            device_id_type=MESH)

    def halo(phase, way, tsub, slot):
        src = (sb, sq)[phase]
        dst = (rb, rq)[phase]
        target = dom - 1 if way == 0 else dom + 1
        return pltpu.make_async_remote_copy(src_ref=src.at[way], dst_ref=dst.at[1 - way, slot],
                                            send_sem=s_halo.at[phase, way, tsub],
                                            recv_sem=r_halo.at[phase, 1 - way, slot],
                                            device_id={"dom": target, "sub": tsub}, device_id_type=MESH)

    def halo_each(phase, act):
        for way in range(2):
            ok = dom > 0 if way == 0 else dom < n_dom - 1

            @pl.when(ok)
            def _():
                for tsub in range(n_sub):
                    act(phase, way, tsub)

    def start_halo(phase):
        def go(phase, way, tsub):
            halo(phase, way, tsub, sub).start()
        halo_each(phase, go)

    def wait_halo_send(phase):
        def go(phase, way, tsub):
            halo(phase, way, tsub, sub).wait_send()
        halo_each(phase, go)

    def wait_halo(phase, ext):
        buf = (rb, rq)[phase]
        for side in range(2):
            there = dom > 0 if side == 0 else dom < n_dom - 1

            @pl.when(there)
            def _():
                for ssub in range(n_sub):
                    halo(phase, 1 - side, 0, ssub).wait_recv()
                lo = 2 * NBR + side * IF
                ext[lo:lo + IF] = buf[side, 0, :IF] + buf[side, 1, :IF]
                if phase == 0:
                    ext_u[lo:lo + IF, :] = buf[side, 0, IF] + buf[side, 1, IF]

            @pl.when(jnp.logical_not(there))
            def _():
                lo = 2 * NBR + side * IF
                ext[lo:lo + IF] = jnp.zeros((IF, 8, 128), F32)
                if phase == 0:
                    ext_u[lo:lo + IF, :] = jnp.zeros((IF, 128), F32)

    def row_copy(row, box, s_sem, r_sem, peer, slot):
        return pltpu.make_async_remote_copy(
            src_ref=row, dst_ref=box.at[slot], send_sem=s_sem.at[peer], recv_sem=r_sem.at[slot],
            device_id={"dom": peer // n_sub, "sub": lax.rem(peer, n_sub)}, device_id_type=MESH)

    def over_peers(act):
        def go(t, c):
            act(lax.rem(me + t, count))
            return c
        lax.fori_loop(1, count, go, 0)

    def start_row(row, box, s_sem, r_sem, value):
        row[...] = value
        over_peers(lambda peer: row_copy(row, box, s_sem, r_sem, peer, me).start())
        box[pl.ds(me, 1)] = value.reshape(1, 1, 128)

    def wait_row(row, box, s_sem, r_sem):
        over_peers(lambda peer: row_copy(row, box, s_sem, r_sem, peer, peer).wait_recv())
        return jnp.sum(box[...], axis=0)

    def wait_row_send(row, box, s_sem, r_sem):
        over_peers(lambda peer: row_copy(row, box, s_sem, r_sem, peer, me).wait_send())

    def grad_copy(peer, slot):
        return pltpu.make_async_remote_copy(
            src_ref=gmsg.at[pl.ds((peer // n_sub) * SLOTS, SLOTS)], dst_ref=rgr.at[slot],
            send_sem=s_g.at[peer], recv_sem=r_g.at[slot],
            device_id={"dom": peer // n_sub, "sub": lax.rem(peer, n_sub)}, device_id_type=MESH)

    partner(0).start()
    partner(1).start()
    start_halo(0)
    ext_b[pl.ds(base, NBR)] = b_ref[...]
    ext_u[pl.ds(base, NBR), :] = u_own[...]

    for load in loads[2:]:
        load.wait()

    def prepare(n, c):
        blocks = [off_ref[n, k] * stiff[k, n] for k in range(NK)] + [diag_ref[n], jnp.zeros((B, B), F32)]
        hi, lo = halves(jnp.concatenate(blocks, axis=1))
        wts[n, :B, :] = hi
        wts[n, B:, :] = lo
        return c

    lax.fori_loop(0, NBR, prepare, 0)

    pr = iota((128, 128), 0)
    pc = iota((128, 128), 1)
    real_r = pr % 8 < NK
    source = jnp.where(real_r, NK * (pr // 8) + pr % 8, -1)[:, :NBR * NK]
    pick = (source == iota((128, NBR * NK), 1)).astype(BF16)
    pair = jnp.where(iota((16, NBR * NK), 0) == 0, jnp.broadcast_to(own_ref[...], (16, NBR * NK)),
                     jnp.broadcast_to(slot_ref[...], (16, NBR * NK)))
    pair = lax.dot_general(pair.astype(F32).astype(BF16), pick, TRANS, preferred_element_type=F32)
    own_row = jnp.where(pc[0:1] % 8 < NK, pair[0:1], -1.0)
    own_col = jnp.sum(jnp.where(pr == pc, own_row, 0.0), axis=1, keepdims=True)
    slot_col = jnp.sum(jnp.where(pr == pc, pair[1:2], 0.0), axis=1, keepdims=True)
    same = (own_col == own_row) & (pr < pc)
    rank_row = jnp.sum(jnp.where(same, 1.0, 0.0), axis=0, keepdims=True)
    dest_row = jnp.where(own_row >= 0.0, own_row * SLOTS + rank_row, -1.0)
    grads[...] = jnp.broadcast_to(slot_col + 1.0, (128, 128))

    lane = iota((8, 128), 1)
    row8 = iota((8, 128), 0)
    low = lane < B

    def gathered(ext, n):
        xs = [ext[cols[k, n]] for k in range(NK)]
        own = ext[base + n]
        pieces = []
        for p in range(NK // 2):
            x0, x1 = xs[2 * p], xs[2 * p + 1]
            top = jnp.where(low, x0, pltpu.roll(x1, B, 1))
            bot = jnp.where(low, pltpu.roll(x0, B, 1), x1)
            pieces.append(jnp.concatenate([top, bot], axis=0))
        own16 = jnp.concatenate([own, pltpu.roll(own, B, 1)], axis=0)
        pieces.append(jnp.where(iota((16, 128), 1) < B, own16, 0.0))
        return jnp.concatenate(pieces, axis=1), own16

    def first(n):
        x, own16 = gathered(ext_b, n)
        hi, lo = halves(x)
        us = [ext_u[pl.ds(cols[k, n], 1), :] for k in range(NK)]
        upieces = []
        for p in range(NK // 2):
            upieces.append(jnp.where((row8 == 2 * p) & low, us[2 * p],
                                     jnp.where((row8 == 2 * p + 1) & ~low, us[2 * p + 1], 0.0)))
        upieces.append(jnp.zeros((8, 128), F32))
        uu = jnp.concatenate(upieces, axis=1)
        uh = uu.astype(BF16).astype(F32)
        u16 = jnp.concatenate([uh, uu - uh], axis=0).astype(BF16)
        lhs = jnp.concatenate([hi, lo, u16], axis=0)
        out = lax.dot_general(lhs, wts[n], TRANS, preferred_element_type=F32)
        t = out[0:16] + out[16:32]
        t = t + pltpu.roll(t, B, 1)
        q_ref[n] = jnp.where(low, t[0:8], t[8:16])
        p = out[32:40] + out[40:48]
        p = jnp.where(low, p + pltpu.roll(p, B, 1), 0.0)
        v = jnp.concatenate([own16, t], axis=0)
        vh = v.astype(BF16)
        vl = (v - vh.astype(F32)).astype(BF16)
        ph = p.astype(BF16).astype(F32)
        p16 = jnp.concatenate([ph, p - ph], axis=0).astype(BF16)
        g = lax.dot_general(p16, jnp.concatenate([vh, vl], axis=0), TRANS, preferred_element_type=F32)
        g = g[0:8] + g[8:16]
        g = g[:, 0:32] + g[:, 32:64]
        grads[pl.ds(pl.multiple_of(n * 8, 8), 8), 0:32] = -g

    def second(n):
        x, _ = gathered(ext_q, n)
        hi, lo = halves(x)
        out = lax.dot_general(jnp.concatenate([hi, lo], axis=0), wts[n], TRANS, preferred_element_type=F32)
        t = out[0:16] + out[16:32]
        t = t + pltpu.roll(t, B, 1)
        w_ref[n] = jnp.where(low, t[0:8], t[8:16])

    def rows(act):
        def go(i, c):
            for j in range(STEP):
                act(i * STEP + j)
            return c
        lax.fori_loop(0, NBR // STEP, go, 0)

    partner(0).wait_recv()
    partner(1).wait_recv()
    wait_halo(0, ext_b)
    rows(first)

    for way in range(2):
        for j in range(IF):
            local = iface[0, way, j] - base
            mine = (local >= 0) & (local < NBR)
            sq[way, j] = jnp.where(mine, q_ref[jnp.clip(local, 0, NBR - 1)], 0.0)
    partner(2).start()
    start_halo(1)
    b = b_ref[...]
    q = q_ref[...]
    ext_q[pl.ds(base, NBR)] = q
    start_row(row1, ar1, s_a1, r_a1, to_row([jnp.sum(b * b, axis=0), jnp.sum(b * q, axis=0)]))

    gh, gl = halves(grads[...])
    for blk in range(n_dom * SLOTS // 128):
        pick2 = (dest_row == (pr + blk * 128).astype(F32)).astype(BF16)
        gmsg[blk * 128:(blk + 1) * 128, :] = (jnp.dot(pick2, gh, preferred_element_type=F32)
                                              + jnp.dot(pick2, gl, preferred_element_type=F32))
    over_peers(lambda peer: grad_copy(peer, me).start())
    rgr[pl.ds(me, 1)] = gmsg[pl.ds(pl.multiple_of(dom * SLOTS, SLOTS), SLOTS), :].reshape(1, SLOTS, 128)

    partner(2).wait_recv()
    wait_halo(1, ext_q)
    rows(second)

    rr, bq = from_row(wait_row(row1, ar1, s_a1, r_a1), 2)
    step1 = rr / bq
    w = w_ref[...]
    r1 = b - step1 * q
    a_r1 = q - step1 * w
    start_row(row2, ar2, s_a2, r_a2, to_row([jnp.sum(r1 * r1, axis=0), jnp.sum(r1 * a_r1, axis=0),
                                             jnp.sum(r1 * q, axis=0), jnp.sum(b * a_r1, axis=0)]))

    over_peers(lambda peer: grad_copy(peer, peer).wait_recv())
    acc = jnp.zeros((2 * R, GEN_DEV), F32)
    for blk in range(count // CHUNK):
        x = rgr[blk * CHUNK:(blk + 1) * CHUNK].reshape(CHUNK * SLOTS, 128)
        hot = (x[:, 32:33] == (iota((CHUNK * SLOTS, GEN_DEV), 1) + 1).astype(F32)).astype(BF16)
        xh, xl = halves(x.T[:2 * R])
        acc = acc + jnp.dot(xh, hot, preferred_element_type=F32) + jnp.dot(xl, hot, preferred_element_type=F32)

    new, m1, m2, m3 = from_row(wait_row(row2, ar2, s_a2, r_a2), 4)
    beta = new / rr
    step2 = new / (m1 + beta * (m2 + m3 + beta * bq))
    adj_ref[...] = step1 * b + step2 * (r1 + beta * b)
    c1 = step1 + step2 * (1.0 + beta)
    c2 = -step2 * step1
    c1 = jnp.concatenate([c1[:, 0:1], c1[:, B:B + 1]], axis=0)
    c2 = jnp.concatenate([c2[:, 0:1], c2[:, B:B + 1]], axis=0)
    gen_ref[...] = c1 * acc[:R] + c2 * acc[R:]

    partner(0).wait_send()
    partner(1).wait_send()
    partner(2).wait_send()
    wait_halo_send(0)
    wait_halo_send(1)
    wait_row_send(row1, ar1, s_a1, r_a1)
    wait_row_send(row2, ar2, s_a2, r_a2)
    over_peers(lambda peer: grad_copy(peer, me).wait_send())


def shards(right_sides, diag_blocks, off_blocks, stiffness, columns, interface, displacement, owners,
           generator_slot):
    n_dom = lax.axis_size("dom")
    n_sub = lax.axis_size("sub")
    count = n_dom * n_sub
    packed = right_sides.reshape(NBR, B, 2, 8).transpose(0, 3, 2, 1).reshape(NBR, 8, 128)
    vmem = pl.BlockSpec(memory_space=pltpu.VMEM)
    dma = pltpu.SemaphoreType.DMA
    ext = 2 * NBR + 2 * IF
    adj, gen = pl.pallas_call(
        functools.partial(kernel, n_dom, n_sub),
        out_shape=(jax.ShapeDtypeStruct((NBR, 8, 128), F32), jax.ShapeDtypeStruct((R, GEN_DEV), F32)),
        in_specs=[pl.BlockSpec(memory_space=pltpu.HBM)] * 8 + [vmem],
        out_specs=(vmem, vmem),
        scratch_shapes=[
            pltpu.SMEM(interface.shape, interface.dtype),
            pltpu.VMEM(displacement.shape, F32),
            pltpu.SMEM(columns.shape[::-1], columns.dtype),
            pltpu.SMEM(stiffness.shape[::-1], F32),
            pltpu.VMEM(diag_blocks.shape, F32),
            pltpu.VMEM(off_blocks.shape, F32),
            pltpu.VMEM(owners.shape[::-1], owners.dtype),
            pltpu.VMEM(generator_slot.shape[::-1], generator_slot.dtype),
            pltpu.VMEM((NBR, 2 * B, 8 * B), BF16),
            pltpu.VMEM((ext, 8, 128), F32),
            pltpu.VMEM((ext, 128), F32),
            pltpu.VMEM((ext, 8, 128), F32),
            pltpu.VMEM((NBR, 8, 128), F32),
            pltpu.VMEM((NBR, 8, 128), F32),
            pltpu.VMEM((NBR, 128), F32),
            pltpu.VMEM((2, IF + 1, 8, 128), F32),
            pltpu.VMEM((2, IF, 8, 128), F32),
            pltpu.VMEM((2, 2, IF + 1, 8, 128), F32),
            pltpu.VMEM((2, 2, IF, 8, 128), F32),
            pltpu.VMEM((128, 128), F32),
            pltpu.VMEM((n_dom * SLOTS, 128), F32),
            pltpu.VMEM((count, SLOTS, 128), F32),
            pltpu.VMEM((count, 1, 128), F32),
            pltpu.VMEM((count, 1, 128), F32),
            pltpu.VMEM((1, 128), F32),
            pltpu.VMEM((1, 128), F32),
            dma((3,)), dma((3,)),
            dma((2, 2, 2)), dma((2, 2, 2)),
            dma((count,)), dma((count,)),
            dma((count,)), dma((count,)),
            dma((count,)), dma((count,)),
            dma((8,)),
        ],
        compiler_params=pltpu.CompilerParams(collective_id=0, has_side_effects=True,
                                             vmem_limit_bytes=60 * 1024 * 1024),
    )(interface, displacement, columns.T, stiffness.T, diag_blocks, off_blocks, owners.T, generator_slot.T, packed)
    adjoint = adj.reshape(NBR, 8, 2, B).transpose(0, 3, 2, 1).reshape(NBR, B * R)
    return adjoint, gen.T


def solution(mesh):
    in_specs = (
        P(("groups", "dom", "sub"), None),
        P(("groups", "dom", "sub"), None, None),
        P(("groups", "dom", "sub"), None, None, None),
        P(("groups", "dom", "sub"), None),
        P(("groups", "dom", "sub"), None),
        P(("groups", "dom"), None, None),
        P(("groups", "dom", "sub"), None),
        P(("groups", "dom", "sub"), None),
        P(("groups", "dom", "sub"), None),
    )
    out_specs = (P(("groups", "dom", "sub"), None), P(("groups", "dom"), None))
    return jax.shard_map(shards, mesh=mesh, in_specs=in_specs, out_specs=out_specs, check_vma=False)
```

```python
import functools
import jax
import jax.numpy as jnp
from jax import lax
from jax.experimental import pallas as pl
from jax.experimental.pallas import tpu as pltpu
from jax.sharding import PartitionSpec as P

B = 64
R = 16
NBR = 16
NK = 6
IF = 8
GEN_DEV = 128
SLOTS = 16
CHUNK = 16

F32 = jnp.float32
BF16 = jnp.bfloat16
MESH = pl.DeviceIdType.MESH
TRANS = (((1,), (1,)), ((), ()))


def iota(shape, dim):
    return lax.broadcasted_iota(jnp.int32, shape, dim)


def halves(x):
    hi = x.astype(BF16)
    lo = (x - hi.astype(F32)).astype(BF16)
    return hi, lo


def to_row(parts):
    lane = iota((8, 128), 1)
    sub = iota((8, 128), 0)
    low = lane < B
    out = jnp.zeros((8, 128), F32)
    for m, part in enumerate(parts):
        s0 = jnp.sum(jnp.where(low, part, 0.0), axis=1, keepdims=True)
        s1 = jnp.sum(jnp.where(low, 0.0, part), axis=1, keepdims=True)
        out = jnp.where(lane % 16 == 2 * m, s0, out)
        out = jnp.where(lane % 16 == 2 * m + 1, s1, out)
    out = jnp.where(sub == lane // 16, out, 0.0)
    return jnp.sum(out, axis=0, keepdims=True)


def from_row(row, count):
    lane = iota((8, 128), 1)
    sub = iota((8, 128), 0)
    own = jnp.where(sub == lane // 16, jnp.broadcast_to(row, (8, 128)), 0.0)
    res = []
    for m in range(count):
        s0 = jnp.sum(jnp.where(lane % 16 == 2 * m, own, 0.0), axis=1, keepdims=True)
        s1 = jnp.sum(jnp.where(lane % 16 == 2 * m + 1, own, 0.0), axis=1, keepdims=True)
        res.append(jnp.where(lane < B, s0, s1))
    return res


def kernel(n_dom, n_sub, *refs):
    hbm, (x_ref, adj_ref, gen_ref), local, rest = refs[:8], refs[8:11], refs[11:19], refs[19:]
    l_sem = rest[-1]
    loads = [pltpu.make_async_copy(hbm[i], local[i], l_sem.at[i]) for i in range(8)]
    for load in loads:
        load.start()
    body(n_dom, n_sub, loads, *local, x_ref, adj_ref, gen_ref, *rest[:-1])


def body(n_dom, n_sub, loads, iface, u_ref, cols, stiff, diag_ref, off_ref, own_ref, slot_ref, x_ref,
         adj_ref, gen_ref, b_ref, wts, ext_b, ext_u, ext_q, q_ref, w_ref, u_own, sb, sq, rb, rq, grads, gmsg, rgr, ar1, ar2, row1, row2,
           s_part, r_part, s_halo, r_halo, s_a1, r_a1, s_a2, r_a2, s_g, r_g):
    dom = lax.axis_index("dom")
    sub = lax.axis_index("sub")
    count = n_dom * n_sub
    me = dom * n_sub + sub
    base = sub * NBR
    other = 1 - sub

    barrier = pltpu.get_barrier_semaphore()

    def greet(t, c):
        peer = lax.rem(me + t, count)
        pl.semaphore_signal(barrier, inc=1, device_id={"dom": peer // n_sub, "sub": lax.rem(peer, n_sub)},
                            device_id_type=MESH)
        return c

    if count > 16:
        lax.fori_loop(1, count, greet, 0)
    else:
        for t in range(1, count):
            greet(t, 0)

    b_ref[...] = jnp.concatenate([x_ref[:, :8, :], x_ref[:, 8:, :]], axis=2)
    loads[0].wait()
    loads[1].wait()
    u = u_ref[...]
    u_own[...] = jnp.concatenate([u, u], axis=1)
    for way in range(2):
        for j in range(IF):
            local = iface[0, way, j] - base
            mine = (local >= 0) & (local < NBR)
            idx = jnp.clip(local, 0, NBR - 1)
            sb[way, j] = jnp.where(mine, b_ref[idx], 0.0)
            sb[way, IF, j:j + 1, :] = jnp.where(mine, u_own[pl.ds(idx, 1), :], 0.0)

    pl.semaphore_wait(barrier, count - 1)

    def partner(which):
        if which == 0:
            src, dst = b_ref, ext_b.at[pl.ds(base, NBR)]
        elif which == 1:
            src, dst = u_own, ext_u.at[pl.ds(base, NBR)]
        else:
            src, dst = q_ref, ext_q.at[pl.ds(base, NBR)]
        return pltpu.make_async_remote_copy(src_ref=src, dst_ref=dst, send_sem=s_part.at[which],
                                            recv_sem=r_part.at[which], device_id={"sub": other},
                                            device_id_type=MESH)

    def halo(phase, way, tsub, slot):
        src = (sb, sq)[phase]
        dst = (rb, rq)[phase]
        target = dom - 1 if way == 0 else dom + 1
        return pltpu.make_async_remote_copy(src_ref=src.at[way], dst_ref=dst.at[1 - way, slot],
                                            send_sem=s_halo.at[phase, way, tsub],
                                            recv_sem=r_halo.at[phase, 1 - way, slot],
                                            device_id={"dom": target, "sub": tsub}, device_id_type=MESH)

    def halo_each(phase, act):
        for way in range(2):
            ok = dom > 0 if way == 0 else dom < n_dom - 1

            @pl.when(ok)
            def _():
                for tsub in range(n_sub):
                    act(phase, way, tsub)

    def start_halo(phase):
        def go(phase, way, tsub):
            halo(phase, way, tsub, sub).start()
        halo_each(phase, go)

    def wait_halo_send(phase):
        def go(phase, way, tsub):
            halo(phase, way, tsub, sub).wait_send()
        halo_each(phase, go)

    def wait_halo(phase, ext):
        buf = (rb, rq)[phase]
        for side in range(2):
            there = dom > 0 if side == 0 else dom < n_dom - 1

            @pl.when(there)
            def _():
                for ssub in range(n_sub):
                    halo(phase, 1 - side, 0, ssub).wait_recv()
                lo = 2 * NBR + side * IF
                ext[lo:lo + IF] = buf[side, 0, :IF] + buf[side, 1, :IF]
                if phase == 0:
                    ext_u[lo:lo + IF, :] = buf[side, 0, IF] + buf[side, 1, IF]

            @pl.when(jnp.logical_not(there))
            def _():
                lo = 2 * NBR + side * IF
                ext[lo:lo + IF] = jnp.zeros((IF, 8, 128), F32)
                if phase == 0:
                    ext_u[lo:lo + IF, :] = jnp.zeros((IF, 128), F32)

    def row_copy(row, box, s_sem, r_sem, peer, slot):
        return pltpu.make_async_remote_copy(
            src_ref=row, dst_ref=box.at[slot], send_sem=s_sem.at[peer], recv_sem=r_sem.at[slot],
            device_id={"dom": peer // n_sub, "sub": lax.rem(peer, n_sub)}, device_id_type=MESH)

    def over_peers(act):
        def go(t, c):
            act(lax.rem(me + t, count))
            return c
        if count > 16:
            lax.fori_loop(1, count, go, 0)
        else:
            for t in range(1, count):
                go(t, 0)

    def start_row(row, box, s_sem, r_sem, value):
        row[...] = value
        over_peers(lambda peer: row_copy(row, box, s_sem, r_sem, peer, me).start())
        box[pl.ds(me, 1)] = value.reshape(1, 1, 128)

    def wait_row(row, box, s_sem, r_sem):
        over_peers(lambda peer: row_copy(row, box, s_sem, r_sem, peer, peer).wait_recv())
        return jnp.sum(box[...], axis=0)

    def wait_row_send(row, box, s_sem, r_sem):
        over_peers(lambda peer: row_copy(row, box, s_sem, r_sem, peer, me).wait_send())

    def grad_copy(peer, slot):
        return pltpu.make_async_remote_copy(
            src_ref=gmsg.at[pl.ds((peer // n_sub) * SLOTS, SLOTS)], dst_ref=rgr.at[slot],
            send_sem=s_g.at[peer], recv_sem=r_g.at[slot],
            device_id={"dom": peer // n_sub, "sub": lax.rem(peer, n_sub)}, device_id_type=MESH)

    partner(0).start()
    partner(1).start()
    start_halo(0)
    ext_b[pl.ds(base, NBR)] = b_ref[...]
    ext_u[pl.ds(base, NBR), :] = u_own[...]

    for load in loads[2:]:
        load.wait()

    def prepare(n, c):
        blocks = [off_ref[n, k] * stiff[k, n] for k in range(NK)] + [diag_ref[n], jnp.zeros((B, B), F32)]
        w = jnp.concatenate(blocks, axis=1)
        wh = w.astype(BF16).astype(F32)
        wts[n] = jnp.concatenate([wh, w - wh], axis=0).T.astype(BF16)
        return c

    lax.fori_loop(0, NBR, prepare, 0)

    pr = iota((128, 128), 0)
    pc = iota((128, 128), 1)
    real_r = pr % 8 < NK
    source = jnp.where(real_r, NK * (pr // 8) + pr % 8, -1)[:, :NBR * NK]
    pick = (source == iota((128, NBR * NK), 1)).astype(BF16)
    pair = jnp.where(iota((16, NBR * NK), 0) == 0, jnp.broadcast_to(own_ref[...], (16, NBR * NK)),
                     jnp.broadcast_to(slot_ref[...], (16, NBR * NK)))
    pair = lax.dot_general(pair.astype(F32).astype(BF16), pick, TRANS, preferred_element_type=F32)
    own_row = jnp.where(pc[0:1] % 8 < NK, pair[0:1], -1.0)
    own_col = jnp.sum(jnp.where(pr == pc, own_row, 0.0), axis=1, keepdims=True)
    slot_col = jnp.sum(jnp.where(pr == pc, pair[1:2], 0.0), axis=1, keepdims=True)
    same = (own_col == own_row) & (pr < pc)
    rank_row = jnp.sum(jnp.where(same, 1.0, 0.0), axis=0, keepdims=True)
    dest_row = jnp.where(own_row >= 0.0, own_row * SLOTS + rank_row, -1.0)
    grads[...] = jnp.broadcast_to(slot_col + 1.0, (128, 128))

    lane = iota((8, 128), 1)
    row8 = iota((8, 128), 0)
    low = lane < B

    def twice(x):
        return jnp.concatenate([x, pltpu.roll(x, B, 1)], axis=0)

    def apply(ext, out_ref, n):
        xs = [ext[cols[k, n]] for k in range(NK)]
        pieces = []
        for p in range(NK // 2):
            x0, x1 = xs[2 * p], xs[2 * p + 1]
            top = jnp.where(low, x0, pltpu.roll(x1, B, 1))
            bot = jnp.where(low, pltpu.roll(x0, B, 1), x1)
            pieces.append(jnp.concatenate([top, bot], axis=0))
        pieces.append(jnp.where(iota((16, 128), 1) < B, twice(ext[base + n]), 0.0))
        hi, lo = halves(jnp.concatenate(pieces, axis=1))
        out = jnp.dot(jnp.concatenate([hi, lo], axis=0), wts[n], preferred_element_type=F32)
        t = out[0:16] + out[16:32]
        t = t + pltpu.roll(t, B, 1)
        out_ref[n] = jnp.where(low, t[0:8], t[8:16])

    def gradients(n):
        us = [ext_u[pl.ds(cols[k, n], 1), :] for k in range(NK)]
        upieces = []
        for p in range(NK // 2):
            upieces.append(jnp.where((row8 == 2 * p) & low, us[2 * p],
                                     jnp.where((row8 == 2 * p + 1) & ~low, us[2 * p + 1], 0.0)))
        upieces.append(jnp.zeros((8, 128), F32))
        uu = jnp.concatenate(upieces, axis=1)
        uh = uu.astype(BF16).astype(F32)
        u16 = jnp.concatenate([uh, uu - uh], axis=0).astype(BF16)
        out = jnp.dot(u16, wts[n], preferred_element_type=F32)
        p = out[0:8] + out[8:16]
        p = jnp.where(low, p + pltpu.roll(p, B, 1), 0.0)
        vh, vl = halves(jnp.concatenate([twice(b_ref[n]), twice(q_ref[n])], axis=0))
        ph = p.astype(BF16).astype(F32)
        p16 = jnp.concatenate([ph, p - ph], axis=0).astype(BF16)
        g = lax.dot_general(p16, jnp.concatenate([vh, vl], axis=0), TRANS, preferred_element_type=F32)
        g = g[0:8] + g[8:16]
        g = g[:, 0:32] + g[:, 32:64]
        grads[n * 8:(n + 1) * 8, 0:32] = -g

    def rows(act):
        for n in range(NBR):
            act(n)

    partner(0).wait_recv()
    partner(1).wait_recv()
    wait_halo(0, ext_b)
    rows(functools.partial(apply, ext_b, q_ref))

    for way in range(2):
        for j in range(IF):
            local = iface[0, way, j] - base
            mine = (local >= 0) & (local < NBR)
            sq[way, j] = jnp.where(mine, q_ref[jnp.clip(local, 0, NBR - 1)], 0.0)
    partner(2).start()
    start_halo(1)
    b = b_ref[...]
    q = q_ref[...]
    ext_q[pl.ds(base, NBR)] = q
    start_row(row1, ar1, s_a1, r_a1, to_row([jnp.sum(b * b, axis=0), jnp.sum(b * q, axis=0)]))

    rows(gradients)
    gh, gl = halves(grads[...])
    for blk in range(n_dom * SLOTS // 128):
        pick2 = (dest_row == (pr + blk * 128).astype(F32)).astype(BF16)
        gmsg[blk * 128:(blk + 1) * 128, :] = (jnp.dot(pick2, gh, preferred_element_type=F32)
                                              + jnp.dot(pick2, gl, preferred_element_type=F32))
    over_peers(lambda peer: grad_copy(peer, me).start())
    rgr[pl.ds(me, 1)] = gmsg[pl.ds(pl.multiple_of(dom * SLOTS, SLOTS), SLOTS), :].reshape(1, SLOTS, 128)

    partner(2).wait_recv()
    wait_halo(1, ext_q)
    rows(functools.partial(apply, ext_q, w_ref))

    rr, bq = from_row(wait_row(row1, ar1, s_a1, r_a1), 2)
    step1 = rr / bq
    w = w_ref[...]
    r1 = b - step1 * q
    a_r1 = q - step1 * w
    start_row(row2, ar2, s_a2, r_a2, to_row([jnp.sum(r1 * r1, axis=0), jnp.sum(r1 * a_r1, axis=0),
                                             jnp.sum(r1 * q, axis=0), jnp.sum(b * a_r1, axis=0)]))

    over_peers(lambda peer: grad_copy(peer, peer).wait_recv())
    acc = jnp.zeros((2 * R, GEN_DEV), F32)
    for blk in range(count // CHUNK):
        x = rgr[blk * CHUNK:(blk + 1) * CHUNK].reshape(CHUNK * SLOTS, 128)
        hot = (x[:, 32:33] == (iota((CHUNK * SLOTS, GEN_DEV), 1) + 1).astype(F32)).astype(BF16)
        xh, xl = halves(x.T[:2 * R])
        acc = acc + jnp.dot(xh, hot, preferred_element_type=F32) + jnp.dot(xl, hot, preferred_element_type=F32)

    new, m1, m2, m3 = from_row(wait_row(row2, ar2, s_a2, r_a2), 4)
    beta = new / rr
    step2 = new / (m1 + beta * (m2 + m3 + beta * bq))
    adjoint = step1 * b + step2 * (r1 + beta * b)
    adj_ref[:, :8, :] = adjoint[:, :, :B]
    adj_ref[:, 8:, :] = adjoint[:, :, B:]
    c1 = step1 + step2 * (1.0 + beta)
    c2 = -step2 * step1
    c1 = jnp.concatenate([c1[:, 0:1], c1[:, B:B + 1]], axis=0)
    c2 = jnp.concatenate([c2[:, 0:1], c2[:, B:B + 1]], axis=0)
    gen_ref[...] = c1 * acc[:R] + c2 * acc[R:]

    partner(0).wait_send()
    partner(1).wait_send()
    partner(2).wait_send()
    wait_halo_send(0)
    wait_halo_send(1)
    wait_row_send(row1, ar1, s_a1, r_a1)
    wait_row_send(row2, ar2, s_a2, r_a2)
    over_peers(lambda peer: grad_copy(peer, me).wait_send())


def shards(right_sides, diag_blocks, off_blocks, stiffness, columns, interface, displacement, owners,
           generator_slot):
    n_dom = lax.axis_size("dom")
    n_sub = lax.axis_size("sub")
    count = n_dom * n_sub
    packed = right_sides.reshape(NBR, B, R).transpose(0, 2, 1)
    vmem = pl.BlockSpec(memory_space=pltpu.VMEM)
    dma = pltpu.SemaphoreType.DMA
    ext = 2 * NBR + 2 * IF
    adj, gen = pl.pallas_call(
        functools.partial(kernel, n_dom, n_sub),
        out_shape=(jax.ShapeDtypeStruct((NBR, R, B), F32), jax.ShapeDtypeStruct((R, GEN_DEV), F32)),
        in_specs=[pl.BlockSpec(memory_space=pltpu.HBM)] * 8 + [vmem],
        out_specs=(vmem, vmem),
        scratch_shapes=[
            pltpu.SMEM(interface.shape, interface.dtype),
            pltpu.VMEM(displacement.shape, F32),
            pltpu.SMEM(columns.shape[::-1], columns.dtype),
            pltpu.SMEM(stiffness.shape[::-1], F32),
            pltpu.VMEM(diag_blocks.shape, F32),
            pltpu.VMEM(off_blocks.shape, F32),
            pltpu.VMEM(owners.shape[::-1], owners.dtype),
            pltpu.VMEM(generator_slot.shape[::-1], generator_slot.dtype),
            pltpu.VMEM((NBR, 8, 128), F32),
            pltpu.VMEM((NBR, 8 * B, 2 * B), BF16),
            pltpu.VMEM((ext, 8, 128), F32),
            pltpu.VMEM((ext, 128), F32),
            pltpu.VMEM((ext, 8, 128), F32),
            pltpu.VMEM((NBR, 8, 128), F32),
            pltpu.VMEM((NBR, 8, 128), F32),
            pltpu.VMEM((NBR, 128), F32),
            pltpu.VMEM((2, IF + 1, 8, 128), F32),
            pltpu.VMEM((2, IF, 8, 128), F32),
            pltpu.VMEM((2, 2, IF + 1, 8, 128), F32),
            pltpu.VMEM((2, 2, IF, 8, 128), F32),
            pltpu.VMEM((128, 128), F32),
            pltpu.VMEM((n_dom * SLOTS, 128), F32),
            pltpu.VMEM((count, SLOTS, 128), F32),
            pltpu.VMEM((count, 1, 128), F32),
            pltpu.VMEM((count, 1, 128), F32),
            pltpu.VMEM((1, 128), F32),
            pltpu.VMEM((1, 128), F32),
            dma((3,)), dma((3,)),
            dma((2, 2, 2)), dma((2, 2, 2)),
            dma((count,)), dma((count,)),
            dma((count,)), dma((count,)),
            dma((count,)), dma((count,)),
            dma((8,)),
        ],
        compiler_params=pltpu.CompilerParams(collective_id=0, has_side_effects=True,
                                             vmem_limit_bytes=60 * 1024 * 1024),
    )(interface, displacement, columns.T, stiffness.T, diag_blocks, off_blocks, owners.T, generator_slot.T, packed)
    adjoint = adj.transpose(0, 2, 1).reshape(NBR, B * R)
    return adjoint, gen.T


def solution(mesh):
    in_specs = (
        P(("groups", "dom", "sub"), None),
        P(("groups", "dom", "sub"), None, None),
        P(("groups", "dom", "sub"), None, None, None),
        P(("groups", "dom", "sub"), None),
        P(("groups", "dom", "sub"), None),
        P(("groups", "dom"), None, None),
        P(("groups", "dom", "sub"), None),
        P(("groups", "dom", "sub"), None),
        P(("groups", "dom", "sub"), None),
    )
    out_specs = (P(("groups", "dom", "sub"), None), P(("groups", "dom"), None))
    return jax.shard_map(shards, mesh=mesh, in_specs=in_specs, out_specs=out_specs, check_vma=False)
```

```python
import functools
import jax
import jax.numpy as jnp
from jax import lax
from jax.experimental import pallas as pl
from jax.experimental.pallas import tpu as pltpu
from jax.sharding import PartitionSpec as P

B = 64
R = 16
NBR = 16
NK = 6
IF = 8
GEN_DEV = 128
SLOTS = 16
CHUNK = 16

F32 = jnp.float32
BF16 = jnp.bfloat16
MESH = pl.DeviceIdType.MESH
TRANS = (((1,), (1,)), ((), ()))


def iota(shape, dim):
    return lax.broadcasted_iota(jnp.int32, shape, dim)


def halves(x):
    hi = x.astype(BF16)
    lo = (x - hi.astype(F32)).astype(BF16)
    return hi, lo


def thirds(x):
    hi, rest = halves(x)
    mid, lo = halves(x - hi.astype(F32))
    return jnp.concatenate([hi, mid, lo], axis=0)


def moved(x, swap):
    src = iota((128, 128), 0)
    dst = iota((128, 128), 1)
    if swap:
        perm = src == (dst % 8) * R + dst // 8
    else:
        perm = dst == (src % 8) * R + src // 8
    y = jnp.dot(thirds(x), perm.astype(BF16), preferred_element_type=F32)
    n = x.shape[0]
    return y[:n] + y[n:2 * n] + y[2 * n:]


def block_swap(xs):
    lane = iota(xs[0].shape, 1)
    xs = list(xs)
    for s in (1, 2, 4):
        first = (lane // 8) % (2 * s) < s
        for i in range(8):
            if i & s == 0:
                x, y = xs[i], xs[i + s]
                xs[i] = jnp.where(first, x, pltpu.roll(y, 8 * s, 1))
                xs[i + s] = jnp.where(first, pltpu.roll(x, 128 - 8 * s, 1), y)
    return xs


def to_row(parts):
    lane = iota((8, 128), 1)
    sub = iota((8, 128), 0)
    low = lane < B
    out = jnp.zeros((8, 128), F32)
    for m, part in enumerate(parts):
        s0 = jnp.sum(jnp.where(low, part, 0.0), axis=1, keepdims=True)
        s1 = jnp.sum(jnp.where(low, 0.0, part), axis=1, keepdims=True)
        out = jnp.where(lane % 16 == 2 * m, s0, out)
        out = jnp.where(lane % 16 == 2 * m + 1, s1, out)
    out = jnp.where(sub == lane // 16, out, 0.0)
    return jnp.sum(out, axis=0, keepdims=True)


def from_row(row, count):
    lane = iota((8, 128), 1)
    sub = iota((8, 128), 0)
    own = jnp.where(sub == lane // 16, jnp.broadcast_to(row, (8, 128)), 0.0)
    res = []
    for m in range(count):
        s0 = jnp.sum(jnp.where(lane % 16 == 2 * m, own, 0.0), axis=1, keepdims=True)
        s1 = jnp.sum(jnp.where(lane % 16 == 2 * m + 1, own, 0.0), axis=1, keepdims=True)
        res.append(jnp.where(lane < B, s0, s1))
    return res


def kernel(n_dom, n_sub, *refs):
    hbm, (adj_ref, gen_ref), local, rest = refs[:9], refs[9:11], refs[11:20], refs[20:]
    l_sem = rest[-1]
    loads = [pltpu.make_async_copy(hbm[i], local[i], l_sem.at[i]) for i in range(9)]
    for load in loads[8:] + loads[:8]:
        load.start()
    body(n_dom, n_sub, loads, *local, adj_ref, gen_ref, *rest[:-1])


def body(n_dom, n_sub, loads, iface, u_ref, cols, stiff, diag_ref, off_ref, own_ref, slot_ref, x_ref,
         adj_ref, gen_ref, b_ref, wts, ext_b, ext_u, ext_q, q_ref, w_ref, u_own, sb, sq, rb, rq, grads, gmsg, rgr, ar1, ar2, row1, row2,
           s_part, r_part, s_halo, r_halo, s_a1, r_a1, s_a2, r_a2, s_g, r_g):
    dom = lax.axis_index("dom")
    sub = lax.axis_index("sub")
    count = n_dom * n_sub
    me = dom * n_sub + sub
    base = sub * NBR
    other = 1 - sub

    barrier = pltpu.get_barrier_semaphore()

    def greet(t, c):
        peer = lax.rem(me + t, count)
        pl.semaphore_signal(barrier, inc=1, device_id={"dom": peer // n_sub, "sub": lax.rem(peer, n_sub)},
                            device_id_type=MESH)
        return c

    if count > 16:
        lax.fori_loop(1, count, greet, 0)
    else:
        for t in range(1, count):
            greet(t, 0)

    loads[8].wait()
    chunks = jnp.concatenate([x_ref[:, c * 128:(c + 1) * 128] for c in range(8)], axis=0)
    chunks = moved(chunks, True)
    for i, z in enumerate(block_swap([chunks[c * NBR:(c + 1) * NBR] for c in range(8)])):
        b_ref[:, i, :] = z
    loads[0].wait()
    loads[1].wait()
    u = u_ref[...]
    u_own[...] = jnp.concatenate([u, u], axis=1)
    for way in range(2):
        for j in range(IF):
            local = iface[0, way, j] - base
            mine = (local >= 0) & (local < NBR)
            idx = jnp.clip(local, 0, NBR - 1)
            sb[way, j] = jnp.where(mine, b_ref[idx], 0.0)
            sb[way, IF, j:j + 1, :] = jnp.where(mine, u_own[pl.ds(idx, 1), :], 0.0)

    pl.semaphore_wait(barrier, count - 1)

    def partner(which):
        if which == 0:
            src, dst = b_ref, ext_b.at[pl.ds(base, NBR)]
        elif which == 1:
            src, dst = u_own, ext_u.at[pl.ds(base, NBR)]
        else:
            src, dst = q_ref, ext_q.at[pl.ds(base, NBR)]
        return pltpu.make_async_remote_copy(src_ref=src, dst_ref=dst, send_sem=s_part.at[which],
                                            recv_sem=r_part.at[which], device_id={"sub": other},
                                            device_id_type=MESH)

    def halo(phase, way, tsub, slot):
        src = (sb, sq)[phase]
        dst = (rb, rq)[phase]
        target = dom - 1 if way == 0 else dom + 1
        return pltpu.make_async_remote_copy(src_ref=src.at[way], dst_ref=dst.at[1 - way, slot],
                                            send_sem=s_halo.at[phase, way, tsub],
                                            recv_sem=r_halo.at[phase, 1 - way, slot],
                                            device_id={"dom": target, "sub": tsub}, device_id_type=MESH)

    def halo_each(phase, act):
        for way in range(2):
            ok = dom > 0 if way == 0 else dom < n_dom - 1

            @pl.when(ok)
            def _():
                for tsub in range(n_sub):
                    act(phase, way, tsub)

    def start_halo(phase):
        def go(phase, way, tsub):
            halo(phase, way, tsub, sub).start()
        halo_each(phase, go)

    def wait_halo_send(phase):
        def go(phase, way, tsub):
            halo(phase, way, tsub, sub).wait_send()
        halo_each(phase, go)

    def wait_halo(phase, ext):
        buf = (rb, rq)[phase]
        for side in range(2):
            there = dom > 0 if side == 0 else dom < n_dom - 1

            @pl.when(there)
            def _():
                for ssub in range(n_sub):
                    halo(phase, 1 - side, 0, ssub).wait_recv()
                lo = 2 * NBR + side * IF
                ext[lo:lo + IF] = buf[side, 0, :IF] + buf[side, 1, :IF]
                if phase == 0:
                    ext_u[lo:lo + IF, :] = buf[side, 0, IF] + buf[side, 1, IF]

            @pl.when(jnp.logical_not(there))
            def _():
                lo = 2 * NBR + side * IF
                ext[lo:lo + IF] = jnp.zeros((IF, 8, 128), F32)
                if phase == 0:
                    ext_u[lo:lo + IF, :] = jnp.zeros((IF, 128), F32)

    def row_copy(row, box, s_sem, r_sem, peer, slot):
        return pltpu.make_async_remote_copy(
            src_ref=row, dst_ref=box.at[slot], send_sem=s_sem.at[peer], recv_sem=r_sem.at[slot],
            device_id={"dom": peer // n_sub, "sub": lax.rem(peer, n_sub)}, device_id_type=MESH)

    def over_peers(act):
        def go(t, c):
            act(lax.rem(me + t, count))
            return c
        if count > 16:
            lax.fori_loop(1, count, go, 0)
        else:
            for t in range(1, count):
                go(t, 0)

    def start_row(row, box, s_sem, r_sem, value):
        row[...] = value
        over_peers(lambda peer: row_copy(row, box, s_sem, r_sem, peer, me).start())
        box[pl.ds(me, 1)] = value.reshape(1, 1, 128)

    def wait_row(row, box, s_sem, r_sem):
        over_peers(lambda peer: row_copy(row, box, s_sem, r_sem, peer, peer).wait_recv())
        return jnp.sum(box[...], axis=0)

    def wait_row_send(row, box, s_sem, r_sem):
        over_peers(lambda peer: row_copy(row, box, s_sem, r_sem, peer, me).wait_send())

    def grad_copy(peer, slot):
        return pltpu.make_async_remote_copy(
            src_ref=gmsg.at[pl.ds((peer // n_sub) * SLOTS, SLOTS)], dst_ref=rgr.at[slot],
            send_sem=s_g.at[peer], recv_sem=r_g.at[slot],
            device_id={"dom": peer // n_sub, "sub": lax.rem(peer, n_sub)}, device_id_type=MESH)

    partner(0).start()
    partner(1).start()
    start_halo(0)
    ext_b[pl.ds(base, NBR)] = b_ref[...]
    ext_u[pl.ds(base, NBR), :] = u_own[...]

    for load in loads[2:8]:
        load.wait()

    def prepare(n, c):
        blocks = [off_ref[n, k] * stiff[k, n] for k in range(NK)] + [diag_ref[n], jnp.zeros((B, B), F32)]
        w = jnp.concatenate(blocks, axis=1)
        wh = w.astype(BF16).astype(F32)
        wts[n] = jnp.concatenate([wh, w - wh], axis=0).T.astype(BF16)
        return c

    lax.fori_loop(0, NBR, prepare, 0)

    pr = iota((128, 128), 0)
    pc = iota((128, 128), 1)
    real_r = pr % 8 < NK
    source = jnp.where(real_r, NK * (pr // 8) + pr % 8, -1)[:, :NBR * NK]
    pick = (source == iota((128, NBR * NK), 1)).astype(BF16)
    pair = jnp.where(iota((16, NBR * NK), 0) == 0, jnp.broadcast_to(own_ref[...], (16, NBR * NK)),
                     jnp.broadcast_to(slot_ref[...], (16, NBR * NK)))
    pair = lax.dot_general(pair.astype(F32).astype(BF16), pick, TRANS, preferred_element_type=F32)
    own_row = jnp.where(pc[0:1] % 8 < NK, pair[0:1], -1.0)
    own_col = jnp.sum(jnp.where(pr == pc, own_row, 0.0), axis=1, keepdims=True)
    slot_col = jnp.sum(jnp.where(pr == pc, pair[1:2], 0.0), axis=1, keepdims=True)
    same = (own_col == own_row) & (pr < pc)
    rank_row = jnp.sum(jnp.where(same, 1.0, 0.0), axis=0, keepdims=True)
    dest_row = jnp.where(own_row >= 0.0, own_row * SLOTS + rank_row, -1.0)
    grads[...] = jnp.broadcast_to(slot_col + 1.0, (128, 128))

    lane = iota((8, 128), 1)
    row8 = iota((8, 128), 0)
    low = lane < B

    def twice(x):
        return jnp.concatenate([x, pltpu.roll(x, B, 1)], axis=0)

    def apply(ext, out_ref, n):
        xs = [ext[cols[k, n]] for k in range(NK)]
        pieces = []
        for p in range(NK // 2):
            x0, x1 = xs[2 * p], xs[2 * p + 1]
            top = jnp.where(low, x0, pltpu.roll(x1, B, 1))
            bot = jnp.where(low, pltpu.roll(x0, B, 1), x1)
            pieces.append(jnp.concatenate([top, bot], axis=0))
        pieces.append(jnp.where(iota((16, 128), 1) < B, twice(ext[base + n]), 0.0))
        hi, lo = halves(jnp.concatenate(pieces, axis=1))
        out = jnp.dot(jnp.concatenate([hi, lo], axis=0), wts[n], preferred_element_type=F32)
        t = out[0:16] + out[16:32]
        t = t + pltpu.roll(t, B, 1)
        out_ref[n] = jnp.where(low, t[0:8], t[8:16])

    def gradients(n):
        us = [ext_u[pl.ds(cols[k, n], 1), :] for k in range(NK)]
        upieces = []
        for p in range(NK // 2):
            upieces.append(jnp.where((row8 == 2 * p) & low, us[2 * p],
                                     jnp.where((row8 == 2 * p + 1) & ~low, us[2 * p + 1], 0.0)))
        upieces.append(jnp.zeros((8, 128), F32))
        uu = jnp.concatenate(upieces, axis=1)
        uh = uu.astype(BF16).astype(F32)
        u16 = jnp.concatenate([uh, uu - uh], axis=0).astype(BF16)
        out = jnp.dot(u16, wts[n], preferred_element_type=F32)
        p = out[0:8] + out[8:16]
        p = jnp.where(low, p + pltpu.roll(p, B, 1), 0.0)
        vh, vl = halves(jnp.concatenate([twice(b_ref[n]), twice(q_ref[n])], axis=0))
        ph = p.astype(BF16).astype(F32)
        p16 = jnp.concatenate([ph, p - ph], axis=0).astype(BF16)
        g = lax.dot_general(p16, jnp.concatenate([vh, vl], axis=0), TRANS, preferred_element_type=F32)
        g = g[0:8] + g[8:16]
        g = g[:, 0:32] + g[:, 32:64]
        grads[n * 8:(n + 1) * 8, 0:32] = -g

    def rows(act):
        for n in range(NBR):
            act(n)

    partner(0).wait_recv()
    partner(1).wait_recv()
    wait_halo(0, ext_b)
    rows(functools.partial(apply, ext_b, q_ref))

    for way in range(2):
        for j in range(IF):
            local = iface[0, way, j] - base
            mine = (local >= 0) & (local < NBR)
            sq[way, j] = jnp.where(mine, q_ref[jnp.clip(local, 0, NBR - 1)], 0.0)
    partner(2).start()
    start_halo(1)
    b = b_ref[...]
    q = q_ref[...]
    ext_q[pl.ds(base, NBR)] = q
    start_row(row1, ar1, s_a1, r_a1, to_row([jnp.sum(b * b, axis=0), jnp.sum(b * q, axis=0)]))

    rows(gradients)
    gh, gl = halves(grads[...])
    for blk in range(n_dom * SLOTS // 128):
        pick2 = (dest_row == (pr + blk * 128).astype(F32)).astype(BF16)
        gmsg[blk * 128:(blk + 1) * 128, :] = (jnp.dot(pick2, gh, preferred_element_type=F32)
                                              + jnp.dot(pick2, gl, preferred_element_type=F32))
    over_peers(lambda peer: grad_copy(peer, me).start())
    rgr[pl.ds(me, 1)] = gmsg[pl.ds(pl.multiple_of(dom * SLOTS, SLOTS), SLOTS), :].reshape(1, SLOTS, 128)

    partner(2).wait_recv()
    wait_halo(1, ext_q)
    rows(functools.partial(apply, ext_q, w_ref))

    rr, bq = from_row(wait_row(row1, ar1, s_a1, r_a1), 2)
    step1 = rr / bq
    w = w_ref[...]
    r1 = b - step1 * q
    a_r1 = q - step1 * w
    start_row(row2, ar2, s_a2, r_a2, to_row([jnp.sum(r1 * r1, axis=0), jnp.sum(r1 * a_r1, axis=0),
                                             jnp.sum(r1 * q, axis=0), jnp.sum(b * a_r1, axis=0)]))

    over_peers(lambda peer: grad_copy(peer, peer).wait_recv())
    acc = jnp.zeros((2 * R, GEN_DEV), F32)
    for blk in range(count // CHUNK):
        x = rgr[blk * CHUNK:(blk + 1) * CHUNK].reshape(CHUNK * SLOTS, 128)
        hot = (x[:, 32:33] == (iota((CHUNK * SLOTS, GEN_DEV), 1) + 1).astype(F32)).astype(BF16)
        xh, xl = halves(x.T[:2 * R])
        acc = acc + jnp.dot(xh, hot, preferred_element_type=F32) + jnp.dot(xl, hot, preferred_element_type=F32)

    new, m1, m2, m3 = from_row(wait_row(row2, ar2, s_a2, r_a2), 4)
    beta = new / rr
    step2 = new / (m1 + beta * (m2 + m3 + beta * bq))
    adjoint = step1 * b + step2 * (r1 + beta * b)
    partner(2).wait_send()
    q_ref[...] = adjoint
    chunks = block_swap([q_ref[:, i, :] for i in range(8)])
    chunks = moved(jnp.concatenate(chunks, axis=0), False)
    for c in range(8):
        adj_ref[:, c * 128:(c + 1) * 128] = chunks[c * NBR:(c + 1) * NBR]
    c1 = step1 + step2 * (1.0 + beta)
    c2 = -step2 * step1
    c1 = jnp.concatenate([c1[:, 0:1], c1[:, B:B + 1]], axis=0)
    c2 = jnp.concatenate([c2[:, 0:1], c2[:, B:B + 1]], axis=0)
    gen_ref[...] = c1 * acc[:R] + c2 * acc[R:]

    partner(0).wait_send()
    partner(1).wait_send()
    wait_halo_send(0)
    wait_halo_send(1)
    wait_row_send(row1, ar1, s_a1, r_a1)
    wait_row_send(row2, ar2, s_a2, r_a2)
    over_peers(lambda peer: grad_copy(peer, me).wait_send())


def shards(right_sides, diag_blocks, off_blocks, stiffness, columns, interface, displacement, owners,
           generator_slot):
    n_dom = lax.axis_size("dom")
    n_sub = lax.axis_size("sub")
    count = n_dom * n_sub
    vmem = pl.BlockSpec(memory_space=pltpu.VMEM)
    dma = pltpu.SemaphoreType.DMA
    ext = 2 * NBR + 2 * IF
    adj, gen = pl.pallas_call(
        functools.partial(kernel, n_dom, n_sub),
        out_shape=(jax.ShapeDtypeStruct((NBR, B * R), F32), jax.ShapeDtypeStruct((R, GEN_DEV), F32)),
        in_specs=[pl.BlockSpec(memory_space=pltpu.HBM)] * 9,
        out_specs=(vmem, vmem),
        scratch_shapes=[
            pltpu.SMEM(interface.shape, interface.dtype),
            pltpu.VMEM(displacement.shape, F32),
            pltpu.SMEM(columns.shape[::-1], columns.dtype),
            pltpu.SMEM(stiffness.shape[::-1], F32),
            pltpu.VMEM(diag_blocks.shape, F32),
            pltpu.VMEM(off_blocks.shape, F32),
            pltpu.VMEM(owners.shape[::-1], owners.dtype),
            pltpu.VMEM(generator_slot.shape[::-1], generator_slot.dtype),
            pltpu.VMEM(right_sides.shape, F32),
            pltpu.VMEM((NBR, 8, 128), F32),
            pltpu.VMEM((NBR, 8 * B, 2 * B), BF16),
            pltpu.VMEM((ext, 8, 128), F32),
            pltpu.VMEM((ext, 128), F32),
            pltpu.VMEM((ext, 8, 128), F32),
            pltpu.VMEM((NBR, 8, 128), F32),
            pltpu.VMEM((NBR, 8, 128), F32),
            pltpu.VMEM((NBR, 128), F32),
            pltpu.VMEM((2, IF + 1, 8, 128), F32),
            pltpu.VMEM((2, IF, 8, 128), F32),
            pltpu.VMEM((2, 2, IF + 1, 8, 128), F32),
            pltpu.VMEM((2, 2, IF, 8, 128), F32),
            pltpu.VMEM((128, 128), F32),
            pltpu.VMEM((n_dom * SLOTS, 128), F32),
            pltpu.VMEM((count, SLOTS, 128), F32),
            pltpu.VMEM((count, 1, 128), F32),
            pltpu.VMEM((count, 1, 128), F32),
            pltpu.VMEM((1, 128), F32),
            pltpu.VMEM((1, 128), F32),
            dma((3,)), dma((3,)),
            dma((2, 2, 2)), dma((2, 2, 2)),
            dma((count,)), dma((count,)),
            dma((count,)), dma((count,)),
            dma((count,)), dma((count,)),
            dma((9,)),
        ],
        compiler_params=pltpu.CompilerParams(collective_id=0, has_side_effects=True,
                                             vmem_limit_bytes=60 * 1024 * 1024),
    )(interface, displacement, columns.T, stiffness.T, diag_blocks, off_blocks, owners.T, generator_slot.T, right_sides)
    return adj, gen.T


def solution(mesh):
    in_specs = (
        P(("groups", "dom", "sub"), None),
        P(("groups", "dom", "sub"), None, None),
        P(("groups", "dom", "sub"), None, None, None),
        P(("groups", "dom", "sub"), None),
        P(("groups", "dom", "sub"), None),
        P(("groups", "dom"), None, None),
        P(("groups", "dom", "sub"), None),
        P(("groups", "dom", "sub"), None),
        P(("groups", "dom", "sub"), None),
    )
    out_specs = (P(("groups", "dom", "sub"), None), P(("groups", "dom"), None))
    return jax.shard_map(shards, mesh=mesh, in_specs=in_specs, out_specs=out_specs, check_vma=False)
```

```python
import functools
import jax
import jax.numpy as jnp
from jax import lax
from jax.experimental import pallas as pl
from jax.experimental.pallas import tpu as pltpu
from jax.sharding import PartitionSpec as P

B = 64
R = 16
NBR = 16
NK = 6
IF = 8
GEN_DEV = 128
SLOTS = 16
CHUNK = 16

F32 = jnp.float32
BF16 = jnp.bfloat16
MESH = pl.DeviceIdType.MESH
TRANS = (((1,), (1,)), ((), ()))


def iota(shape, dim):
    return lax.broadcasted_iota(jnp.int32, shape, dim)


def halves(x):
    hi = x.astype(BF16)
    lo = (x - hi.astype(F32)).astype(BF16)
    return hi, lo


def thirds(x):
    hi, rest = halves(x)
    mid, lo = halves(x - hi.astype(F32))
    return jnp.concatenate([hi, mid, lo], axis=0)


def moved(x, swap):
    src = iota((128, 128), 0)
    dst = iota((128, 128), 1)
    if swap:
        perm = src == (dst % 8) * R + dst // 8
    else:
        perm = dst == (src % 8) * R + src // 8
    y = jnp.dot(thirds(x), perm.astype(BF16), preferred_element_type=F32)
    n = x.shape[0]
    return y[:n] + y[n:2 * n] + y[2 * n:]


def block_swap(xs):
    lane = iota(xs[0].shape, 1)
    xs = list(xs)
    for s in (1, 2, 4):
        first = (lane // 8) % (2 * s) < s
        for i in range(8):
            if i & s == 0:
                x, y = xs[i], xs[i + s]
                xs[i] = jnp.where(first, x, pltpu.roll(y, 8 * s, 1))
                xs[i + s] = jnp.where(first, pltpu.roll(x, 128 - 8 * s, 1), y)
    return xs


def to_row(parts):
    lane = iota((8, 128), 1)
    sub = iota((8, 128), 0)
    low = lane < B
    out = jnp.zeros((8, 128), F32)
    for m, part in enumerate(parts):
        s0 = jnp.sum(jnp.where(low, part, 0.0), axis=1, keepdims=True)
        s1 = jnp.sum(jnp.where(low, 0.0, part), axis=1, keepdims=True)
        out = jnp.where(lane % 16 == 2 * m, s0, out)
        out = jnp.where(lane % 16 == 2 * m + 1, s1, out)
    out = jnp.where(sub == lane // 16, out, 0.0)
    return jnp.sum(out, axis=0, keepdims=True)


def from_row(row, count):
    lane = iota((8, 128), 1)
    sub = iota((8, 128), 0)
    own = jnp.where(sub == lane // 16, jnp.broadcast_to(row, (8, 128)), 0.0)
    res = []
    for m in range(count):
        s0 = jnp.sum(jnp.where(lane % 16 == 2 * m, own, 0.0), axis=1, keepdims=True)
        s1 = jnp.sum(jnp.where(lane % 16 == 2 * m + 1, own, 0.0), axis=1, keepdims=True)
        res.append(jnp.where(lane < B, s0, s1))
    return res


def kernel(n_dom, n_sub, *refs):
    hbm, (adj_ref, gen_ref), local, rest = refs[:9], refs[9:11], refs[11:20], refs[20:]
    l_sem = rest[-1]
    loads = [pltpu.make_async_copy(hbm[i], local[i], l_sem.at[i]) for i in range(9)]
    for load in loads[8:] + loads[:8]:
        load.start()
    body(n_dom, n_sub, loads, *local, adj_ref, gen_ref, *rest[:-1])


def body(n_dom, n_sub, loads, iface, u_ref, cols, stiff, diag_ref, off_ref, own_ref, slot_ref, x_ref,
         adj_ref, gen_ref, b_ref, wts, ext_b, ext_u, ext_q, q_ref, w_ref, u_own, sb, sq, rb, rq, grads, gmsg, rgr, ar1, ar2, row1, row2,
           s_part, r_part, s_halo, r_halo, s_a1, r_a1, s_a2, r_a2, s_g, r_g):
    dom = lax.axis_index("dom")
    sub = lax.axis_index("sub")
    count = n_dom * n_sub
    me = dom * n_sub + sub
    base = sub * NBR
    other = 1 - sub

    barrier = pltpu.get_barrier_semaphore()

    def greet(t, c):
        peer = lax.rem(me + t, count)
        pl.semaphore_signal(barrier, inc=1, device_id={"dom": peer // n_sub, "sub": lax.rem(peer, n_sub)},
                            device_id_type=MESH)
        return c

    if count > 16:
        lax.fori_loop(1, count, greet, 0)
    else:
        for t in range(1, count):
            greet(t, 0)

    loads[8].wait()
    chunks = jnp.concatenate([x_ref[:, c * 128:(c + 1) * 128] for c in range(8)], axis=0)
    chunks = moved(chunks, True)
    for i, z in enumerate(block_swap([chunks[c * NBR:(c + 1) * NBR] for c in range(8)])):
        b_ref[:, i, :] = z
    loads[0].wait()
    loads[1].wait()
    u = u_ref[...]
    u_own[...] = jnp.concatenate([u, u], axis=1)
    for way in range(2):
        for j in range(IF):
            local = iface[0, way, j] - base
            mine = (local >= 0) & (local < NBR)
            idx = jnp.clip(local, 0, NBR - 1)
            sb[way, j] = jnp.where(mine, b_ref[idx], 0.0)
            sb[way, IF, j:j + 1, :] = jnp.where(mine, u_own[pl.ds(idx, 1), :], 0.0)

    pl.semaphore_wait(barrier, count - 1)

    def partner(which):
        if which == 0:
            src, dst = b_ref, ext_b.at[pl.ds(base, NBR)]
        elif which == 1:
            src, dst = u_own, ext_u.at[pl.ds(base, NBR)]
        else:
            src, dst = q_ref, ext_q.at[pl.ds(base, NBR)]
        return pltpu.make_async_remote_copy(src_ref=src, dst_ref=dst, send_sem=s_part.at[which],
                                            recv_sem=r_part.at[which], device_id={"sub": other},
                                            device_id_type=MESH)

    def halo(phase, way, tsub, slot):
        src = (sb, sq)[phase]
        dst = (rb, rq)[phase]
        target = dom - 1 if way == 0 else dom + 1
        return pltpu.make_async_remote_copy(src_ref=src.at[way], dst_ref=dst.at[1 - way, slot],
                                            send_sem=s_halo.at[phase, way, tsub],
                                            recv_sem=r_halo.at[phase, 1 - way, slot],
                                            device_id={"dom": target, "sub": tsub}, device_id_type=MESH)

    def halo_each(phase, act):
        for way in range(2):
            ok = dom > 0 if way == 0 else dom < n_dom - 1

            @pl.when(ok)
            def _():
                for tsub in range(n_sub):
                    act(phase, way, tsub)

    def start_halo(phase):
        def go(phase, way, tsub):
            halo(phase, way, tsub, sub).start()
        halo_each(phase, go)

    def wait_halo_send(phase):
        def go(phase, way, tsub):
            halo(phase, way, tsub, sub).wait_send()
        halo_each(phase, go)

    def wait_halo(phase, ext):
        buf = (rb, rq)[phase]
        for side in range(2):
            there = dom > 0 if side == 0 else dom < n_dom - 1

            @pl.when(there)
            def _():
                for ssub in range(n_sub):
                    halo(phase, 1 - side, 0, ssub).wait_recv()
                lo = 2 * NBR + side * IF
                ext[lo:lo + IF] = buf[side, 0, :IF] + buf[side, 1, :IF]
                if phase == 0:
                    ext_u[lo:lo + IF, :] = buf[side, 0, IF] + buf[side, 1, IF]

            @pl.when(jnp.logical_not(there))
            def _():
                lo = 2 * NBR + side * IF
                ext[lo:lo + IF] = jnp.zeros((IF, 8, 128), F32)
                if phase == 0:
                    ext_u[lo:lo + IF, :] = jnp.zeros((IF, 128), F32)

    def row_copy(row, box, s_sem, r_sem, peer, slot):
        return pltpu.make_async_remote_copy(
            src_ref=row, dst_ref=box.at[slot], send_sem=s_sem.at[peer], recv_sem=r_sem.at[slot],
            device_id={"dom": peer // n_sub, "sub": lax.rem(peer, n_sub)}, device_id_type=MESH)

    def over_peers(act):
        def go(t, c):
            act(lax.rem(me + t, count))
            return c
        if count > 16:
            lax.fori_loop(1, count, go, 0)
        else:
            for t in range(1, count):
                go(t, 0)

    def start_row(row, box, s_sem, r_sem, value):
        row[...] = value
        over_peers(lambda peer: row_copy(row, box, s_sem, r_sem, peer, me).start())
        box[pl.ds(me, 1)] = value.reshape(1, 1, 128)

    def wait_row(row, box, s_sem, r_sem):
        over_peers(lambda peer: row_copy(row, box, s_sem, r_sem, peer, peer).wait_recv())
        return jnp.sum(box[...], axis=0)

    def wait_row_send(row, box, s_sem, r_sem):
        over_peers(lambda peer: row_copy(row, box, s_sem, r_sem, peer, me).wait_send())

    def grad_copy(peer, slot):
        return pltpu.make_async_remote_copy(
            src_ref=gmsg.at[pl.ds((peer // n_sub) * SLOTS, SLOTS)], dst_ref=rgr.at[slot],
            send_sem=s_g.at[peer], recv_sem=r_g.at[slot],
            device_id={"dom": peer // n_sub, "sub": lax.rem(peer, n_sub)}, device_id_type=MESH)

    start_halo(0)
    partner(0).start()
    partner(1).start()
    ext_b[pl.ds(base, NBR)] = b_ref[...]
    ext_u[pl.ds(base, NBR), :] = u_own[...]

    for load in loads[2:8]:
        load.wait()

    def prepare(n, c):
        blocks = [off_ref[n, k] * stiff[k, n] for k in range(NK)] + [diag_ref[n], jnp.zeros((B, B), F32)]
        w = jnp.concatenate(blocks, axis=1)
        wh = w.astype(BF16).astype(F32)
        wts[n] = jnp.concatenate([wh, w - wh], axis=0).T.astype(BF16)
        return c

    lax.fori_loop(0, NBR, prepare, 0)

    pr = iota((128, 128), 0)
    pc = iota((128, 128), 1)
    real_r = pr % 8 < NK
    source = jnp.where(real_r, NK * (pr // 8) + pr % 8, -1)[:, :NBR * NK]
    pick = (source == iota((128, NBR * NK), 1)).astype(BF16)
    pair = jnp.where(iota((16, NBR * NK), 0) == 0, jnp.broadcast_to(own_ref[...], (16, NBR * NK)),
                     jnp.broadcast_to(slot_ref[...], (16, NBR * NK)))
    pair = lax.dot_general(pair.astype(F32).astype(BF16), pick, TRANS, preferred_element_type=F32)
    own_row = jnp.where(pc[0:1] % 8 < NK, pair[0:1], -1.0)
    own_col = jnp.sum(jnp.where(pr == pc, own_row, 0.0), axis=1, keepdims=True)
    slot_col = jnp.sum(jnp.where(pr == pc, pair[1:2], 0.0), axis=1, keepdims=True)
    same = (own_col == own_row) & (pr < pc)
    rank_row = jnp.sum(jnp.where(same, 1.0, 0.0), axis=0, keepdims=True)
    dest_row = jnp.where(own_row >= 0.0, own_row * SLOTS + rank_row, -1.0)
    grads[...] = jnp.broadcast_to(slot_col + 1.0, (128, 128))

    lane = iota((8, 128), 1)
    row8 = iota((8, 128), 0)
    low = lane < B

    def twice(x):
        return jnp.concatenate([x, pltpu.roll(x, B, 1)], axis=0)

    def apply(ext, out_ref, n):
        xs = [ext[cols[k, n]] for k in range(NK)]
        pieces = []
        for p in range(NK // 2):
            x0, x1 = xs[2 * p], xs[2 * p + 1]
            top = jnp.where(low, x0, pltpu.roll(x1, B, 1))
            bot = jnp.where(low, pltpu.roll(x0, B, 1), x1)
            pieces.append(jnp.concatenate([top, bot], axis=0))
        pieces.append(jnp.where(iota((16, 128), 1) < B, twice(ext[base + n]), 0.0))
        hi, lo = halves(jnp.concatenate(pieces, axis=1))
        out = jnp.dot(jnp.concatenate([hi, lo], axis=0), wts[n], preferred_element_type=F32)
        t = out[0:16] + out[16:32]
        t = t + pltpu.roll(t, B, 1)
        out_ref[n] = jnp.where(low, t[0:8], t[8:16])

    def gradients(n):
        us = [ext_u[pl.ds(cols[k, n], 1), :] for k in range(NK)]
        upieces = []
        for p in range(NK // 2):
            upieces.append(jnp.where((row8 == 2 * p) & low, us[2 * p],
                                     jnp.where((row8 == 2 * p + 1) & ~low, us[2 * p + 1], 0.0)))
        upieces.append(jnp.zeros((8, 128), F32))
        uu = jnp.concatenate(upieces, axis=1)
        uh = uu.astype(BF16).astype(F32)
        u16 = jnp.concatenate([uh, uu - uh], axis=0).astype(BF16)
        out = jnp.dot(u16, wts[n], preferred_element_type=F32)
        p = out[0:8] + out[8:16]
        p = jnp.where(low, p + pltpu.roll(p, B, 1), 0.0)
        vh, vl = halves(jnp.concatenate([twice(b_ref[n]), twice(q_ref[n])], axis=0))
        ph = p.astype(BF16).astype(F32)
        p16 = jnp.concatenate([ph, p - ph], axis=0).astype(BF16)
        g = lax.dot_general(p16, jnp.concatenate([vh, vl], axis=0), TRANS, preferred_element_type=F32)
        g = g[0:8] + g[8:16]
        g = g[:, 0:32] + g[:, 32:64]
        grads[n * 8:(n + 1) * 8, 0:32] = -g

    def rows(act):
        for n in range(NBR):
            act(n)

    partner(0).wait_recv()
    partner(1).wait_recv()
    wait_halo(0, ext_b)
    rows(functools.partial(apply, ext_b, q_ref))

    for way in range(2):
        for j in range(IF):
            local = iface[0, way, j] - base
            mine = (local >= 0) & (local < NBR)
            sq[way, j] = jnp.where(mine, q_ref[jnp.clip(local, 0, NBR - 1)], 0.0)
    start_halo(1)
    partner(2).start()
    b = b_ref[...]
    q = q_ref[...]
    ext_q[pl.ds(base, NBR)] = q
    start_row(row1, ar1, s_a1, r_a1, to_row([jnp.sum(b * b, axis=0), jnp.sum(b * q, axis=0)]))

    rows(gradients)
    gh, gl = halves(grads[...])
    for blk in range(n_dom * SLOTS // 128):
        pick2 = (dest_row == (pr + blk * 128).astype(F32)).astype(BF16)
        gmsg[blk * 128:(blk + 1) * 128, :] = (jnp.dot(pick2, gh, preferred_element_type=F32)
                                              + jnp.dot(pick2, gl, preferred_element_type=F32))
    over_peers(lambda peer: grad_copy(peer, me).start())
    rgr[pl.ds(me, 1)] = gmsg[pl.ds(pl.multiple_of(dom * SLOTS, SLOTS), SLOTS), :].reshape(1, SLOTS, 128)

    partner(2).wait_recv()
    wait_halo(1, ext_q)
    rows(functools.partial(apply, ext_q, w_ref))

    rr, bq = from_row(wait_row(row1, ar1, s_a1, r_a1), 2)
    step1 = rr / bq
    w = w_ref[...]
    r1 = b - step1 * q
    a_r1 = q - step1 * w
    start_row(row2, ar2, s_a2, r_a2, to_row([jnp.sum(r1 * r1, axis=0), jnp.sum(r1 * a_r1, axis=0),
                                             jnp.sum(r1 * q, axis=0), jnp.sum(b * a_r1, axis=0)]))

    over_peers(lambda peer: grad_copy(peer, peer).wait_recv())
    acc = jnp.zeros((2 * R, GEN_DEV), F32)
    for blk in range(count // CHUNK):
        x = rgr[blk * CHUNK:(blk + 1) * CHUNK].reshape(CHUNK * SLOTS, 128)
        hot = (x[:, 32:33] == (iota((CHUNK * SLOTS, GEN_DEV), 1) + 1).astype(F32)).astype(BF16)
        xh, xl = halves(x.T[:2 * R])
        acc = acc + jnp.dot(xh, hot, preferred_element_type=F32) + jnp.dot(xl, hot, preferred_element_type=F32)

    new, m1, m2, m3 = from_row(wait_row(row2, ar2, s_a2, r_a2), 4)
    beta = new / rr
    step2 = new / (m1 + beta * (m2 + m3 + beta * bq))
    adjoint = step1 * b + step2 * (r1 + beta * b)
    partner(2).wait_send()
    q_ref[...] = adjoint
    chunks = block_swap([q_ref[:, i, :] for i in range(8)])
    chunks = moved(jnp.concatenate(chunks, axis=0), False)
    for c in range(8):
        adj_ref[:, c * 128:(c + 1) * 128] = chunks[c * NBR:(c + 1) * NBR]
    c1 = step1 + step2 * (1.0 + beta)
    c2 = -step2 * step1
    c1 = jnp.concatenate([c1[:, 0:1], c1[:, B:B + 1]], axis=0)
    c2 = jnp.concatenate([c2[:, 0:1], c2[:, B:B + 1]], axis=0)
    gen_ref[...] = c1 * acc[:R] + c2 * acc[R:]

    partner(0).wait_send()
    partner(1).wait_send()
    wait_halo_send(0)
    wait_halo_send(1)
    wait_row_send(row1, ar1, s_a1, r_a1)
    wait_row_send(row2, ar2, s_a2, r_a2)
    over_peers(lambda peer: grad_copy(peer, me).wait_send())


def shards(right_sides, diag_blocks, off_blocks, stiffness, columns, interface, displacement, owners,
           generator_slot):
    n_dom = lax.axis_size("dom")
    n_sub = lax.axis_size("sub")
    count = n_dom * n_sub
    vmem = pl.BlockSpec(memory_space=pltpu.VMEM)
    dma = pltpu.SemaphoreType.DMA
    ext = 2 * NBR + 2 * IF
    adj, gen = pl.pallas_call(
        functools.partial(kernel, n_dom, n_sub),
        out_shape=(jax.ShapeDtypeStruct((NBR, B * R), F32), jax.ShapeDtypeStruct((R, GEN_DEV), F32)),
        in_specs=[pl.BlockSpec(memory_space=pltpu.HBM)] * 9,
        out_specs=(vmem, vmem),
        scratch_shapes=[
            pltpu.SMEM(interface.shape, interface.dtype),
            pltpu.VMEM(displacement.shape, F32),
            pltpu.SMEM(columns.shape[::-1], columns.dtype),
            pltpu.SMEM(stiffness.shape[::-1], F32),
            pltpu.VMEM(diag_blocks.shape, F32),
            pltpu.VMEM(off_blocks.shape, F32),
            pltpu.VMEM(owners.shape[::-1], owners.dtype),
            pltpu.VMEM(generator_slot.shape[::-1], generator_slot.dtype),
            pltpu.VMEM(right_sides.shape, F32),
            pltpu.VMEM((NBR, 8, 128), F32),
            pltpu.VMEM((NBR, 8 * B, 2 * B), BF16),
            pltpu.VMEM((ext, 8, 128), F32),
            pltpu.VMEM((ext, 128), F32),
            pltpu.VMEM((ext, 8, 128), F32),
            pltpu.VMEM((NBR, 8, 128), F32),
            pltpu.VMEM((NBR, 8, 128), F32),
            pltpu.VMEM((NBR, 128), F32),
            pltpu.VMEM((2, IF + 1, 8, 128), F32),
            pltpu.VMEM((2, IF, 8, 128), F32),
            pltpu.VMEM((2, 2, IF + 1, 8, 128), F32),
            pltpu.VMEM((2, 2, IF, 8, 128), F32),
            pltpu.VMEM((128, 128), F32),
            pltpu.VMEM((n_dom * SLOTS, 128), F32),
            pltpu.VMEM((count, SLOTS, 128), F32),
            pltpu.VMEM((count, 1, 128), F32),
            pltpu.VMEM((count, 1, 128), F32),
            pltpu.VMEM((1, 128), F32),
            pltpu.VMEM((1, 128), F32),
            dma((3,)), dma((3,)),
            dma((2, 2, 2)), dma((2, 2, 2)),
            dma((count,)), dma((count,)),
            dma((count,)), dma((count,)),
            dma((count,)), dma((count,)),
            dma((9,)),
        ],
        compiler_params=pltpu.CompilerParams(collective_id=0, has_side_effects=True,
                                             vmem_limit_bytes=60 * 1024 * 1024),
    )(interface, displacement, columns.T, stiffness.T, diag_blocks, off_blocks, owners.T, generator_slot.T, right_sides)
    return adj, gen.T


def solution(mesh):
    in_specs = (
        P(("groups", "dom", "sub"), None),
        P(("groups", "dom", "sub"), None, None),
        P(("groups", "dom", "sub"), None, None, None),
        P(("groups", "dom", "sub"), None),
        P(("groups", "dom", "sub"), None),
        P(("groups", "dom"), None, None),
        P(("groups", "dom", "sub"), None),
        P(("groups", "dom", "sub"), None),
        P(("groups", "dom", "sub"), None),
    )
    out_specs = (P(("groups", "dom", "sub"), None), P(("groups", "dom"), None))
    return jax.shard_map(shards, mesh=mesh, in_specs=in_specs, out_specs=out_specs, check_vma=False)
```
